256 devices in a mesh: dp: 32 (over z_hi, y, core), band: 8 (over x, z_lo).
Axes of the slice: x: 4, y: 4, z: 8 (z_hi: 4, z_lo: 2; z = z_hi * 2 + z_lo), core: 2. Of those that a mesh axis runs over, the one named last changes fastest.
Arguments:
- radiance: bfloat16 [32, 280, 32, 128], P('dp', 'band'), may hold values from -6 to 6
- kernel: bfloat16 [280, 7, 7], P('band'), may hold values from -0.875 to 0.875
- w_first: bfloat16 [280, 64], replicated, may hold values from -0.375 to 0.375
- w_mid: bfloat16 [64, 64], replicated, may hold values from -0.75 to 0.75
- w_out: bfloat16 [64, 280], replicated, may hold values from -0.75 to 0.75
- target: bfloat16 [32, 280, 32, 128], P('dp', None, 'band'), may hold values from -6 to 6
- mask: int32 [32, 32, 128], P('dp', 'band'), may hold values 0 or 1
Outputs:
- grad_kernel: float32 [280, 7, 7], P('band')
- grad_first: float32 [280, 64], replicated
- grad_mid: float32 [64, 64], replicated
- grad_out: float32 [64, 280], replicated
The draws below stay inside these ranges and needn't reach their ends.
All inputs are finite; a program needn't handle non-finite values. No bound on the sum of `mask` on one device may be relied on, other than what follows from the above.
Results may differ from the reference program's by a relative error of at most 0.00056.
Values may be sent and summed in bfloat16 or wider, within the bound.
No kernel may reach another device: no remote copies, remote signals or barrier semaphores. Data moves between devices by JAX's collectives and lax.ppermute only.
A program may use at most 64 MiB of HBM per device.

```python
import math
import jax
import jax.numpy as jnp
from jax import lax

BANDS = 280
CH = 64
KS = 7
H = 32
W = 128
CROPS = 32


def plant(result, key, smallest, largest):
    place = [jax.random.randint(jax.random.fold_in(key, axis), (), 0, length) for axis, length in enumerate(result.shape)]
    main_axis = result.shape.index(max(result.shape))
    next_to = place[:main_axis] + [(place[main_axis] + 1) % result.shape[main_axis]] + place[main_axis + 1:]
    return result.at[tuple(place)].set(smallest).at[tuple(next_to)].set(largest)


def shard_levels(key, shape, split, low, largest):
    def one(dim, blocks):
        draws = jax.random.uniform(jax.random.fold_in(jax.random.fold_in(key, 6), dim), (blocks,), jnp.float32, low / len(split), largest / len(split))
        return jnp.repeat(jnp.exp(draws), shape[dim] // blocks).reshape((-1,) + (1,) * (len(shape) - dim - 1))

    loudness = one(*split[0])
    for cut in split[1:]:
        loudness = loudness * one(*cut)
    return loudness


def bell_draw(own_key, dims, width, limit, pieces=(), kind=jnp.bfloat16):
    gain = shard_levels(own_key, dims, pieces, -0.22, 0.18) if pieces else 1.0
    result = jax.random.normal(own_key, dims, jnp.float32) * width * gain
    return jnp.minimum(jnp.maximum(result, -limit), limit).astype(kind)


def setup_inputs(seed: int = 0) -> dict:
    key_list = jax.random.split(jax.random.key(seed), 8)
    radiance = bell_draw(key_list[0], (CROPS, BANDS, H, W), 1.0, 6.0, ((0, 32), (1, 8)))
    kernel = bell_draw(key_list[1], (BANDS, KS, KS), (KS * KS) ** -0.5, 0.875, ((0, 8),))
    w_first = bell_draw(key_list[2], (BANDS, CH), BANDS ** -0.5, 0.375)
    w_mid = bell_draw(key_list[3], (CH, CH), CH ** -0.5, 0.75)
    w_out = bell_draw(key_list[4], (CH, BANDS), CH ** -0.5, 0.75)
    target = bell_draw(key_list[5], (CROPS, BANDS, H, W), 1.0, 6.0, ((0, 32), (2, 8)))
    mask = plant((jax.random.randint(key_list[6], (CROPS, H, W), 0, 4) < 3).astype(jnp.int32), jax.random.fold_in(key_list[6], 1), 0, 1)
    return {"radiance": radiance, "kernel": kernel, "w_first": w_first, "w_mid": w_mid, "w_out": w_out, "target": target, "mask": mask}


def spatial(image, kernel):
    out = lax.conv_general_dilated(image[None], kernel[:, None], (1, 1), ((3, 3), (3, 3)), dimension_numbers=('NCHW', 'OIHW', 'NCHW'), feature_group_count=image.shape[0], preferred_element_type=jnp.float32)
    return out[0]

def kernel_slope(image, slope):
    out = lax.conv_general_dilated(image[None], slope[:, None], (1, 1), ((3, 3), (3, 3)), dimension_numbers=('NCHW', 'OIHW', 'NCHW'), feature_group_count=image.shape[0], preferred_element_type=jnp.float32)
    return out[0]

def silu_slope(value):
    sig = jax.nn.sigmoid(value)
    return sig * (1.0 + value * (1.0 - sig))

def reference(radiance, kernel, w_first, w_mid, w_out, target, mask):
    scale = 1.0 / math.sqrt(CROPS * H * W)
    first = w_first.astype(jnp.float32)
    middle = w_mid.astype(jnp.float32)
    outer = w_out.astype(jnp.float32)

    def one_crop(items):
        image, wanted, valid = items
        filtered = spatial(image, kernel).astype(jnp.bfloat16)
        z_first = jnp.einsum('bhw,bc->chw', filtered.astype(jnp.float32), first)
        hid_first = jax.nn.silu(z_first).astype(jnp.bfloat16)
        z_mid = jnp.einsum('chw,cd->dhw', hid_first.astype(jnp.float32), middle)
        hid_mid = (hid_first.astype(jnp.float32) + jax.nn.silu(z_mid)).astype(jnp.bfloat16)
        predicted = jnp.einsum('chw,co->ohw', hid_mid.astype(jnp.float32), outer)
        err = (2.0 * scale * valid.astype(jnp.float32)[None] * (predicted - wanted.astype(jnp.float32))).astype(jnp.bfloat16)
        errf = err.astype(jnp.float32)
        grad_out = jnp.einsum('chw,ohw->co', hid_mid.astype(jnp.float32), errf)
        d_mid = jnp.einsum('co,ohw->chw', outer, errf)
        dz_mid = (d_mid * silu_slope(z_mid)).astype(jnp.bfloat16)
        grad_mid = jnp.einsum('chw,dhw->cd', hid_first.astype(jnp.float32), dz_mid.astype(jnp.float32))
        d_first = d_mid + jnp.einsum('cd,dhw->chw', middle, dz_mid.astype(jnp.float32))
        dz_first = (d_first * silu_slope(z_first)).astype(jnp.bfloat16)
        grad_first = jnp.einsum('bhw,chw->bc', filtered.astype(jnp.float32), dz_first.astype(jnp.float32))
        slope = jnp.einsum('bc,chw->bhw', first, dz_first.astype(jnp.float32)).astype(jnp.bfloat16)
        grad_kernel = kernel_slope(image, slope)
        return (grad_kernel, grad_first, grad_mid, grad_out)
    parts = lax.map(one_crop, (radiance, target, mask))
    return (lax.optimization_barrier(jnp.sum(parts[0], axis=0)), lax.optimization_barrier(jnp.sum(parts[1], axis=0)), lax.optimization_barrier(jnp.sum(parts[2], axis=0)), lax.optimization_barrier(jnp.sum(parts[3], axis=0)))
```

```python
import functools
import math

import jax
import jax.numpy as jnp
from jax import lax
from jax.experimental import pallas as pl
from jax.experimental.pallas import tpu as pltpu
from jax.sharding import PartitionSpec as P

F32 = jnp.float32
BF16 = jnp.bfloat16
LANES = 128


def round_up(value, step):
    return -(-value // step) * step


def silu_slope(value, sig):
    return sig * (1.0 + value * (1.0 - sig))


def lane_row(shape):
    return (lax.broadcasted_iota(jnp.int32, shape, 1), lax.broadcasted_iota(jnp.int32, shape, 0))


def near_diagonal(rows, half, upside_down=False):
    lane, row = lane_row((rows, LANES))
    if upside_down:
        row = rows - 1 - row
    away = lane % rows - row
    return (away >= -half) & (away <= half)


def shifted_columns(image, ks):
    half = ks // 2
    lane, _ = lane_row(image.shape)
    parts = []
    for j in range(ks):
        step = j - half
        if step == 0:
            parts.append(image)
            continue
        moved = pltpu.roll(image, (-step) % LANES, 1)
        inside = lane < LANES - step if step > 0 else lane >= -step
        parts.append(jnp.where(inside, moved, 0.0))
    groups = round_up(ks * image.shape[0], LANES) // image.shape[0]
    parts += [jnp.zeros_like(image)] * (groups - ks)
    return jnp.concatenate(parts, axis=0).astype(BF16)


def spatial_kernel(rad_ref, taps_ref, out_ref, spread_ref, rows_ref):
    bands, rows, _ = rad_ref.shape
    ks = taps_ref.shape[0]
    half = ks // 2
    per = LANES // rows
    tiles = spread_ref.shape[1] // LANES
    lane, row = lane_row((ks, tiles * LANES))
    spread = jnp.zeros((bands, tiles * LANES), F32)
    for i in range(ks):
        home = (row // per) * LANES + ((row % per) * rows + (i - half) + LANES) % LANES
        hot = (lane == home).astype(BF16)
        spread += lax.dot_general(taps_ref[i], hot, (((0,), (0,)), ((), ())), preferred_element_type=F32)
    spread_ref[...] = spread
    keep = near_diagonal(rows, half)

    for b in range(bands):
        image = rad_ref[b].astype(F32)
        columns = shifted_columns(image, ks)
        mats = []
        for t in range(tiles):
            line = spread_ref[b:b + 1, t * LANES:(t + 1) * LANES]
            wide = jnp.broadcast_to(line, (rows, LANES))
            wide = pltpu.roll(wide, 0, 1, stride=1, stride_axis=0)
            mats.append(jnp.where(keep, wide, 0.0))
        mix = jnp.concatenate(mats, axis=1).astype(BF16)
        out = jnp.dot(mix, columns, preferred_element_type=F32)
        rows_ref[pl.ds(b, rows, stride=bands), :] = out
    peers, size, _ = out_ref.shape
    count = rows * bands // peers
    for d in range(peers):
        out_ref[d, 0:count, :] = rows_ref[d * count:(d + 1) * count, :].astype(BF16)
        if size > count:
            out_ref[d, count:size, :] = jnp.zeros((size - count, LANES), BF16)


def net_kernel(spec_ref, first_ref, mid_ref, outer_ref, want_ref, valid_ref, out_ref, a_ref, b_ref, g_ref, *, scale):
    peers, size, _ = spec_ref.shape
    ch, total = first_ref.shape
    rows = valid_ref.shape[0]
    bands = total // peers
    first = first_ref[...]
    middle = mid_ref[...]
    outer = outer_ref[...]
    a_ref[0:rows * total, :] = want_ref[...].astype(F32)
    wanted = jnp.concatenate([a_ref[pl.ds(r, total, stride=rows), :] for r in range(rows)], axis=1)
    for s in range(peers):
        a_ref[s * size:(s + 1) * size, :] = spec_ref[s].astype(F32)
    for s in range(peers):
        for r in range(rows):
            src = s * size + r * bands
            dst = r * total + s * bands
            b_ref[dst:dst + bands, :] = a_ref[src:src + bands, :]
    spectra = jnp.concatenate([b_ref[r * total:(r + 1) * total, :].astype(BF16) for r in range(rows)], axis=1)

    def mm(x, y, dx, dy):
        return lax.dot_general(x, y, (((dx,), (dy,)), ((), ())), preferred_element_type=F32)

    z_first = mm(first, spectra, 1, 0)
    sig_first = jax.nn.sigmoid(z_first)
    hid_first = (z_first * sig_first).astype(BF16)
    z_mid = mm(middle, hid_first, 0, 0)
    sig_mid = jax.nn.sigmoid(z_mid)
    hid_mid = (hid_first.astype(F32) + z_mid * sig_mid).astype(BF16)
    predicted = mm(outer, hid_mid, 0, 0)
    valid = jnp.concatenate([valid_ref[r:r + 1, :] for r in range(rows)], axis=1).astype(F32)
    err = (2.0 * scale * valid * (predicted - wanted)).astype(BF16)
    d_mid = mm(outer, err, 1, 0)
    dz_mid = (d_mid * silu_slope(z_mid, sig_mid)).astype(BF16)
    d_first = d_mid + mm(middle, dz_mid, 1, 0)
    dz_first = (d_first * silu_slope(z_first, sig_first)).astype(BF16)
    slope = mm(first, dz_first, 0, 0)
    for r in range(rows):
        b_ref[r * total:(r + 1) * total, :] = slope[:, r * LANES:(r + 1) * LANES]
    for s in range(peers):
        for r in range(rows):
            src = r * total + s * bands
            dst = s * size + (rows - 1 - r) * bands
            a_ref[dst:dst + bands, :] = b_ref[src:src + bands, :]
    used = rows * bands
    for s in range(peers):
        if size > used:
            a_ref[s * size + used:(s + 1) * size, :] = jnp.zeros((size - used, LANES), F32)
        out_ref[s, 0:size, :] = a_ref[s * size:(s + 1) * size, :].astype(BF16)
    wide = round_up(total, LANES)
    g_ref[:, 0:total] = mm(dz_first, spectra, 1, 1)
    g_ref[:, wide - ch:wide] = mm(hid_first, dz_mid, 1, 1)
    g_ref[:, wide:wide + total] = mm(hid_mid, err, 1, 1)
    g_ref[:, wide + total:2 * wide] = jnp.zeros((ch, wide - total), F32)
    gap = wide - ch - total
    if gap > 0:
        g_ref[:, total:wide - ch] = jnp.zeros((ch, gap), F32)
    share = ch // peers
    tiles = 2 * wide // LANES
    for s in range(peers):
        piece = jnp.concatenate(
            [g_ref[s * share:(s + 1) * share, t * LANES:(t + 1) * LANES] for t in range(tiles)], axis=0
        )
        high = piece.astype(BF16)
        low = (piece - high.astype(F32)).astype(BF16)
        n = tiles * share
        out_ref[s, size:size + n, :] = high
        out_ref[s, size + n:size + 2 * n, :] = low


def kernel_grad_kernel(rad_ref, in_ref, out_ref, rows_ref, acc_ref, *, ks, size):
    bands, rows, _ = rad_ref.shape
    half = ks // 2
    peers = in_ref.shape[0]
    count = rows * bands // peers
    n = (in_ref.shape[1] - size) // 2
    total = jnp.zeros((n, LANES), F32)
    for s in range(peers):
        total += in_ref[s, size:size + n, :].astype(F32) + in_ref[s, size + n:size + 2 * n, :].astype(F32)
    out_ref[0:n, :] = total
    for s in range(peers):
        back = peers - 1 - s
        rows_ref[back * count:(back + 1) * count, :] = in_ref[s, 0:size, :].astype(F32)[0:count]
    keep = near_diagonal(rows, half, upside_down=True)
    per = LANES // rows
    tiles = -(-ks // per)

    for b in range(bands):
        columns = shifted_columns(rad_ref[b].astype(F32), ks)
        slope = rows_ref[pl.ds(b, rows, stride=bands), :].astype(BF16)
        full = lax.dot_general(slope, columns, (((1,), (1,)), ((), ())), preferred_element_type=F32)
        acc = jnp.zeros((8, LANES), F32)
        for t in range(tiles):
            part = jnp.where(keep, full[:, t * LANES:(t + 1) * LANES], 0.0)
            part = pltpu.roll(part, LANES + 1 - rows, 1, stride=1, stride_axis=0)
            part = jnp.sum(part.reshape(rows // 8, 8, LANES), axis=0)
            if t:
                part = pltpu.roll(part, t * (ks + 1), 1)
            acc += part
        acc_ref[b * 8:(b + 1) * 8, :] = acc
    result = acc_ref[pl.ds(0, bands, stride=8), :]
    for k in range(1, 8):
        result += acc_ref[pl.ds(k, bands, stride=8), :]
    out_ref[n:n + bands, :] = result
    rest = out_ref.shape[0] - n - bands
    if rest:
        out_ref[n + bands:n + bands + rest, :] = jnp.zeros((rest, LANES), F32)


def final_kernel(all_ref, own_ref, gk_ref, gf_ref, gm_ref, go_ref, t_ref, g_ref):
    ks, _, bands = gk_ref.shape
    half = ks // 2
    peers, n, _ = all_ref.shape
    ch, total = gf_ref.shape
    share = ch // peers
    wide = round_up(total, LANES)
    rows = LANES // 4
    per = LANES // rows
    t_ref[...] = own_ref[...].T
    for i in range(ks):
        for j in range(ks):
            lane = ((j % per) * rows + (j // per) * (ks + 1) + (i - half)) % LANES
            gk_ref[i, j:j + 1, :] = t_ref[lane:lane + 1, 0:bands]
    for s in range(peers):
        for t in range(n // share):
            g_ref[s * share:(s + 1) * share, t * LANES:(t + 1) * LANES] = all_ref[s, t * share:(t + 1) * share, :]
    gf_ref[...] = g_ref[:, 0:total]
    gm_ref[...] = g_ref[:, wide - ch:wide]
    go_ref[...] = g_ref[:, wide:wide + total]


def exchange(block, axis):
    return lax.all_to_all(block, axis, split_axis=0, concat_axis=0, tiled=True)


def reduce_far(value, axis):
    members = lax.axis_size(axis)

    def other(block, flip):
        return lax.ppermute(block, axis, [(i, i ^ flip) for i in range(members)])

    value = value + other(value, 1)
    step = 2
    while step < members:
        value = (value + other(value, step)) + (other(value, 2 * step) + other(value, 3 * step))
        step *= 4
    return value


def on_device(radiance, kernel, w_first, w_mid, w_out, target, mask):
    image = radiance[0]
    bands, rows_all, width = image.shape
    ks = kernel.shape[1]
    peers = lax.axis_size("band")
    rows = mask.shape[1]
    total, ch = w_first.shape
    scale = 1.0 / math.sqrt(lax.axis_size("dp") * rows_all * width)
    size = round_up(rows * bands, 16)
    taps = jnp.transpose(kernel, (1, 2, 0))
    first = jnp.transpose(w_first, (1, 0))
    wanted = target[0].reshape(total * rows, width)
    spread_wide = round_up(ks * rows_all, LANES)
    filtered = pl.pallas_call(
        spatial_kernel,
        out_shape=jax.ShapeDtypeStruct((peers, size, width), BF16),
        scratch_shapes=[pltpu.VMEM((bands, spread_wide), F32), pltpu.VMEM((bands * rows_all, width), F32)],
        name="spatial",
    )(image, taps)
    spectra = exchange(filtered, "band")
    wide = round_up(total, LANES)
    share_rows = 2 * wide // LANES * (ch // peers)
    packed = pl.pallas_call(
        functools.partial(net_kernel, scale=scale),
        out_shape=jax.ShapeDtypeStruct((peers, size + 2 * share_rows, width), BF16),
        scratch_shapes=[
            pltpu.VMEM((peers * size, width), F32),
            pltpu.VMEM((rows * total, width), F32),
            pltpu.VMEM((ch, 2 * wide), F32),
        ],
        name="net",
    )(spectra, first, w_mid, w_out, wanted, mask[0])
    packed = exchange(packed, "band")
    bands_up = round_up(bands, 8)
    sums = pl.pallas_call(
        functools.partial(kernel_grad_kernel, ks=ks, size=size),
        out_shape=jax.ShapeDtypeStruct((share_rows + bands_up, width), F32),
        scratch_shapes=[pltpu.VMEM((bands * rows_all, width), F32), pltpu.VMEM((bands * 8, width), F32)],
        name="kernel_grad",
    )(image, packed)
    sums = reduce_far(sums, "dp")
    shared = exchange(jnp.broadcast_to(sums[None, :share_rows], (peers, share_rows, width)), "band")
    grad_kernel, grad_first, grad_mid, grad_out = pl.pallas_call(
        final_kernel,
        out_shape=(
            jax.ShapeDtypeStruct((ks, ks, bands), F32),
            jax.ShapeDtypeStruct((ch, total), F32),
            jax.ShapeDtypeStruct((ch, ch), F32),
            jax.ShapeDtypeStruct((ch, total), F32),
        ),
        scratch_shapes=[pltpu.VMEM((LANES, bands_up), F32), pltpu.VMEM((ch, 2 * wide), F32)],
        name="final",
    )(shared, sums[share_rows:])
    return (jnp.transpose(grad_kernel, (2, 0, 1)), jnp.transpose(grad_first, (1, 0)), grad_mid, grad_out)


def solution(mesh):
    in_specs = (
        P("dp", "band", None, None),
        P("band", None, None),
        P(),
        P(),
        P(),
        P("dp", None, "band", None),
        P("dp", "band", None),
    )
    out_specs = (P("band", None, None), P(), P(), P())
    return jax.shard_map(on_device, mesh=mesh, in_specs=in_specs, out_specs=out_specs, check_vma=False)
```

```python
import functools
import math

import jax
import jax.numpy as jnp
from jax import lax
from jax.experimental import pallas as pl
from jax.experimental.pallas import tpu as pltpu
from jax.sharding import PartitionSpec as P

F32 = jnp.float32
BF16 = jnp.bfloat16
LANES = 128
LOADS = 5
SMALL = pltpu.CompilerParams(vmem_limit_bytes=16 << 20)


def round_up(value, step):
    return -(-value // step) * step


def silu_slope(value, sig):
    return sig * (1.0 + value * (1.0 - sig))


def lane_row(shape):
    return (lax.broadcasted_iota(jnp.int32, shape, 1), lax.broadcasted_iota(jnp.int32, shape, 0))


def near_diagonal(rows, half, upside_down=False):
    lane, row = lane_row((rows, LANES))
    if upside_down:
        row = rows - 1 - row
    away = lane % rows - row
    return (away >= -half) & (away <= half)


def shifted_columns(image, ks):
    half = ks // 2
    lane, _ = lane_row(image.shape)
    parts = []
    for j in range(ks):
        step = j - half
        if step == 0:
            parts.append(image)
            continue
        moved = pltpu.roll(image, (-step) % LANES, 1)
        inside = lane < LANES - step if step > 0 else lane >= -step
        parts.append(jnp.where(inside, moved, jnp.zeros_like(moved)))
    groups = round_up(ks * image.shape[0], LANES) // image.shape[0]
    parts += [jnp.zeros_like(image)] * (groups - ks)
    return jnp.concatenate(parts, axis=0)


def spatial_kernel(*refs):
    more = (len(refs) - 8) // 2
    rad_hbm, taps_hbm = refs[:2]
    far = refs[2:2 + more]
    out_ref, rad_ref = refs[2 + more:4 + more]
    kept = refs[4 + more:4 + 2 * more]
    taps_ref, spread_ref, rows_ref, sems = refs[4 + 2 * more:]
    bands, rows, _ = rad_ref.shape
    chunk = bands // LOADS
    taps_copy = pltpu.make_async_copy(taps_hbm, taps_ref, sems.at[LOADS])
    taps_copy.start()
    loads = []
    for k in range(LOADS):
        part = pl.ds(k * chunk, chunk)
        loads.append(pltpu.make_async_copy(rad_hbm.at[part], rad_ref.at[part], sems.at[k]))
        loads[-1].start()
    others = []
    for k in range(more):
        others.append(pltpu.make_async_copy(far[k], kept[k], sems.at[LOADS + 1 + k]))
        others[-1].start()
    ks = taps_ref.shape[0]
    half = ks // 2
    per = LANES // rows
    tiles = spread_ref.shape[1] // LANES
    lane, row = lane_row((ks, tiles * LANES))
    taps_copy.wait()
    spread = jnp.zeros((bands, tiles * LANES), F32)
    for i in range(ks):
        home = (row // per) * LANES + ((row % per) * rows + (i - half) + LANES) % LANES
        hot = (lane == home).astype(BF16)
        spread += lax.dot_general(taps_ref[i], hot, (((0,), (0,)), ((), ())), preferred_element_type=F32)
    spread_ref[...] = spread
    keep = near_diagonal(rows, half)
    for b in range(bands):
        if b % chunk == 0:
            loads[b // chunk].wait()
        columns = shifted_columns(rad_ref[b], ks)
        mats = []
        for t in range(tiles):
            line = spread_ref[b:b + 1, t * LANES:(t + 1) * LANES]
            wide = jnp.broadcast_to(line, (rows, LANES))
            wide = pltpu.roll(wide, 0, 1, stride=1, stride_axis=0)
            mats.append(jnp.where(keep, wide, 0.0))
        mix = jnp.concatenate(mats, axis=1).astype(BF16)
        out = jnp.dot(mix, columns, preferred_element_type=F32)
        rows_ref[pl.ds(b, rows, stride=bands), :] = out
    peers, size, _ = out_ref.shape
    count = rows * bands // peers
    for d in range(peers):
        out_ref[d, 0:count, :] = rows_ref[d * count:(d + 1) * count, :].astype(BF16)
        if size > count:
            out_ref[d, count:size, :] = jnp.zeros((size - count, LANES), BF16)
    for copy in others:
        copy.wait()


def net_kernel(spec_ref, first_ref, mid_ref, outer_ref, want_ref, valid_ref, out_ref, a_ref, b_ref, g_ref, *, scale):
    peers, size, _ = spec_ref.shape
    ch, total = first_ref.shape
    rows = valid_ref.shape[0]
    bands = total // peers
    first = first_ref[...]
    middle = mid_ref[...]
    outer = outer_ref[...]
    a_ref[0:rows * total, :] = want_ref[...].astype(F32)
    wanted = jnp.concatenate([a_ref[pl.ds(r, total, stride=rows), :] for r in range(rows)], axis=1)
    for s in range(peers):
        a_ref[s * size:(s + 1) * size, :] = spec_ref[s].astype(F32)
    for s in range(peers):
        for r in range(rows):
            src = s * size + r * bands
            dst = r * total + s * bands
            b_ref[dst:dst + bands, :] = a_ref[src:src + bands, :]
    spectra = jnp.concatenate([b_ref[r * total:(r + 1) * total, :].astype(BF16) for r in range(rows)], axis=1)

    def mm(x, y, dx, dy):
        return lax.dot_general(x, y, (((dx,), (dy,)), ((), ())), preferred_element_type=F32)

    z_first = mm(first, spectra, 1, 0)
    sig_first = jax.nn.sigmoid(z_first)
    hid_first = (z_first * sig_first).astype(BF16)
    z_mid = mm(middle, hid_first, 0, 0)
    sig_mid = jax.nn.sigmoid(z_mid)
    hid_mid = (hid_first.astype(F32) + z_mid * sig_mid).astype(BF16)
    predicted = mm(outer, hid_mid, 0, 0)
    valid = jnp.concatenate([valid_ref[r:r + 1, :] for r in range(rows)], axis=1).astype(F32)
    err = (2.0 * scale * valid * (predicted - wanted)).astype(BF16)
    d_mid = mm(outer, err, 1, 0)
    dz_mid = (d_mid * silu_slope(z_mid, sig_mid)).astype(BF16)
    d_first = d_mid + mm(middle, dz_mid, 1, 0)
    dz_first = (d_first * silu_slope(z_first, sig_first)).astype(BF16)
    slope = mm(first, dz_first, 0, 0)
    for r in range(rows):
        b_ref[r * total:(r + 1) * total, :] = slope[:, r * LANES:(r + 1) * LANES]
    for s in range(peers):
        for r in range(rows):
            src = r * total + s * bands
            dst = s * size + (rows - 1 - r) * bands
            a_ref[dst:dst + bands, :] = b_ref[src:src + bands, :]
    used = rows * bands
    for s in range(peers):
        if size > used:
            a_ref[s * size + used:(s + 1) * size, :] = jnp.zeros((size - used, LANES), F32)
        out_ref[s, 0:size, :] = a_ref[s * size:(s + 1) * size, :].astype(BF16)
    wide = g_ref.shape[1]
    used = 2 * total + ch
    g_ref[:, 0:total] = mm(dz_first, spectra, 1, 1)
    g_ref[:, total:2 * total] = mm(hid_mid, err, 1, 1)
    g_ref[:, 2 * total:used] = mm(hid_first, dz_mid, 1, 1)
    if wide > used:
        g_ref[:, used:wide] = jnp.zeros((ch, wide - used), F32)
    share = ch // peers
    tiles = wide // LANES
    for s in range(peers):
        piece = jnp.concatenate(
            [g_ref[s * share:(s + 1) * share, t * LANES:(t + 1) * LANES] for t in range(tiles)], axis=0
        )
        high = piece.astype(BF16)
        low = (piece - high.astype(F32)).astype(BF16)
        n = tiles * share
        out_ref[s, size:size + n, :] = high
        out_ref[s, size + n:size + 2 * n, :] = low


def kernel_grad_kernel(rad_ref, in_ref, out_ref, rows_ref, acc_ref, *, ks, size):
    bands, rows, _ = rad_ref.shape
    peers = in_ref.shape[0]
    half = ks // 2
    count = rows * bands // peers
    n = (in_ref.shape[1] - size) // 2
    total = jnp.zeros((n, LANES), F32)
    for s in range(peers):
        total += in_ref[s, size:size + n, :].astype(F32) + in_ref[s, size + n:size + 2 * n, :].astype(F32)
    out_ref[0:n, :] = total
    for s in range(peers):
        back = peers - 1 - s
        rows_ref[back * count:(back + 1) * count, :] = in_ref[s, 0:size, :].astype(F32)[0:count]
    keep = near_diagonal(rows, half, upside_down=True)
    per = LANES // rows
    tiles = -(-ks // per)
    for b in range(bands):
        slope = rows_ref[pl.ds(b, rows, stride=bands), :].astype(BF16)
        columns = shifted_columns(rad_ref[b], ks)
        full = lax.dot_general(slope, columns, (((1,), (1,)), ((), ())), preferred_element_type=F32)
        acc = jnp.zeros((8, LANES), F32)
        for t in range(tiles):
            part = jnp.where(keep, full[:, t * LANES:(t + 1) * LANES], 0.0)
            part = pltpu.roll(part, LANES + 1 - rows, 1, stride=1, stride_axis=0)
            part = jnp.sum(part.reshape(rows // 8, 8, LANES), axis=0)
            if t:
                part = pltpu.roll(part, t * (ks + 1), 1)
            acc += part
        acc_ref[b * 8:(b + 1) * 8, :] = acc
    result = acc_ref[pl.ds(0, bands, stride=8), :]
    for k in range(1, 8):
        result += acc_ref[pl.ds(k, bands, stride=8), :]
    out_ref[n:n + bands, :] = result
    rest = out_ref.shape[0] - n - bands
    if rest:
        out_ref[n + bands:n + bands + rest, :] = jnp.zeros((rest, LANES), F32)


def join_kernel(a_ref, b_ref, c_ref, d_ref, all_ref, own_ref):
    value = (a_ref[...] + b_ref[...]) + (c_ref[...] + d_ref[...])
    peers, n, _ = all_ref.shape
    for s in range(peers):
        all_ref[s] = value[0:n]
    own_ref[...] = value[n:]


def final_kernel(all_ref, own_ref, gk_ref, gf_ref, gm_ref, go_ref, t_ref, g_ref, *, rows):
    ks, _, bands = gk_ref.shape
    half = ks // 2
    per = LANES // rows
    t_ref[...] = own_ref[...].T
    for i in range(ks):
        for j in range(ks):
            lane = ((j % per) * rows + (j // per) * (ks + 1) + (i - half)) % LANES
            gk_ref[i, j:j + 1, :] = t_ref[lane:lane + 1, 0:bands]
    peers, n, _ = all_ref.shape
    ch, total = gf_ref.shape
    share = ch // peers
    for s in range(peers):
        for t in range(n // share):
            g_ref[s * share:(s + 1) * share, t * LANES:(t + 1) * LANES] = all_ref[s, t * share:(t + 1) * share, :]
    gf_ref[...] = g_ref[:, 0:total]
    go_ref[...] = g_ref[:, total:2 * total]
    gm_ref[...] = g_ref[:, 2 * total:2 * total + ch]


def near(*arrays):
    return [pltpu.with_memory_space_constraint(a, pltpu.VMEM) for a in arrays]


def spots(count):
    return [pl.BlockSpec(memory_space=pltpu.VMEM)] * count


def exchange(block, axis):
    return lax.all_to_all(block, axis, split_axis=0, concat_axis=0, tiled=True)


def group_parts(value, axis, stride):
    members = lax.axis_size(axis)

    def other(flip):
        return lax.ppermute(value, axis, [(i, i ^ flip) for i in range(members)])

    return (value, other(stride), other(2 * stride), other(3 * stride))


def on_device(radiance, kernel, w_first, w_mid, w_out, target, mask):
    image = radiance[0]
    bands, rows_all, width = image.shape
    ks = kernel.shape[1]
    peers = lax.axis_size("band")
    crops = lax.axis_size("dp")
    rows = mask.shape[1]
    total, ch = w_first.shape
    scale = 1.0 / math.sqrt(crops * rows_all * width)
    size = round_up(rows * bands, 16)
    taps = jnp.transpose(kernel, (1, 2, 0))
    first = jnp.transpose(w_first, (1, 0))
    wanted = target[0].reshape(total * rows, width)
    spread_wide = round_up(ks * rows_all, LANES)
    params = (image, taps, first, w_mid, w_out, wanted, mask[0])
    filtered, image, first, w_mid, w_out, wanted, valid = pl.pallas_call(
        spatial_kernel,
        in_specs=[pl.BlockSpec(memory_space=pltpu.HBM)] * len(params),
        out_specs=spots(len(params)),
        out_shape=(pltpu.VMEM((peers, size, width), BF16),)
        + tuple(pltpu.VMEM(p.shape, p.dtype) for p in (image,) + params[2:]),
        scratch_shapes=[
            pltpu.VMEM(taps.shape, BF16),
            pltpu.VMEM((bands, spread_wide), F32),
            pltpu.VMEM((bands * rows_all, width), F32),
            pltpu.SemaphoreType.DMA((LOADS + len(params),)),
        ],
        compiler_params=SMALL,
        name="spatial",
    )(*[pltpu.with_memory_space_constraint(p, pltpu.HBM) for p in params])
    spectra = exchange(filtered, "band")
    wide = round_up(2 * total + ch, LANES)
    share_rows = wide // LANES * (ch // peers)
    packed = pl.pallas_call(
        functools.partial(net_kernel, scale=scale),
        in_specs=spots(6),
        out_specs=spots(1)[0],
        out_shape=pltpu.VMEM((peers, size + 2 * share_rows, width), BF16),
        scratch_shapes=[
            pltpu.VMEM((peers * size, width), F32),
            pltpu.VMEM((rows * total, width), F32),
            pltpu.VMEM((ch, wide), F32),
        ],
        compiler_params=SMALL,
        name="net",
    )(*near(spectra, first, w_mid, w_out, wanted, valid))
    packed = exchange(packed, "band")
    bands_up = round_up(bands, 8)
    sums = pl.pallas_call(
        functools.partial(kernel_grad_kernel, ks=ks, size=size),
        in_specs=spots(2),
        out_specs=spots(1)[0],
        out_shape=pltpu.VMEM((share_rows + bands_up, width), F32),
        scratch_shapes=[pltpu.VMEM((bands * rows_all, width), F32), pltpu.VMEM((bands * 8, width), F32)],
        compiler_params=SMALL,
        name="kernel_grad",
    )(*near(image, packed))
    sums = sums + lax.ppermute(sums, "dp", [(i, i ^ 1) for i in range(crops)])
    if crops == 32:
        a, b, c, d = group_parts(sums, "dp", 2)
        sums = (a + b) + (c + d)
        parts = group_parts(sums, "dp", 8)
    else:
        parts = (sums,) + (jnp.zeros_like(sums),) * 3
    shared, own = pl.pallas_call(
        join_kernel,
        in_specs=spots(4),
        out_specs=spots(2),
        out_shape=(pltpu.VMEM((peers, share_rows, width), F32), pltpu.VMEM((bands_up, width), F32)),
        compiler_params=SMALL,
        name="join",
    )(*near(*parts))
    shared = exchange(shared, "band")
    grad_kernel, grad_first, grad_mid, grad_out = pl.pallas_call(
        functools.partial(final_kernel, rows=rows_all),
        in_specs=spots(2),
        out_shape=(
            jax.ShapeDtypeStruct((ks, ks, bands), F32),
            jax.ShapeDtypeStruct((ch, total), F32),
            jax.ShapeDtypeStruct((ch, ch), F32),
            jax.ShapeDtypeStruct((ch, total), F32),
        ),
        scratch_shapes=[pltpu.VMEM((LANES, bands_up), F32), pltpu.VMEM((ch, wide), F32)],
        compiler_params=SMALL,
        name="final",
    )(*near(shared, own))
    return (jnp.transpose(grad_kernel, (2, 0, 1)), jnp.transpose(grad_first, (1, 0)), grad_mid, grad_out)


def solution(mesh):
    in_specs = (
        P("dp", "band", None, None),
        P("band", None, None),
        P(),
        P(),
        P(),
        P("dp", None, "band", None),
        P("dp", "band", None),
    )
    out_specs = (P("band", None, None), P(), P(), P())
    return jax.shard_map(on_device, mesh=mesh, in_specs=in_specs, out_specs=out_specs, check_vma=False)
```

```python
import functools
import math

import jax
import jax.numpy as jnp
from jax import lax
from jax.experimental import pallas as pl
from jax.experimental.pallas import tpu as pltpu
from jax.sharding import PartitionSpec as P

F32 = jnp.float32
BF16 = jnp.bfloat16
LANES = 128
LOADS = 1
SMALL = pltpu.CompilerParams(vmem_limit_bytes=16 << 20)


def round_up(value, step):
    return -(-value // step) * step


def silu_slope(value, sig):
    return sig * (1.0 + value * (1.0 - sig))


def lane_row(shape):
    return (lax.broadcasted_iota(jnp.int32, shape, 1), lax.broadcasted_iota(jnp.int32, shape, 0))


def near_diagonal(rows, half, upside_down=False):
    lane, row = lane_row((rows, LANES))
    if upside_down:
        row = rows - 1 - row
    away = lane % rows - row
    return (away >= -half) & (away <= half)


def shifted_columns(image, ks):
    half = ks // 2
    lane, _ = lane_row(image.shape)
    parts = []
    for j in range(ks):
        step = j - half
        if step == 0:
            parts.append(image)
            continue
        moved = pltpu.roll(image, (-step) % LANES, 1)
        inside = lane < LANES - step if step > 0 else lane >= -step
        parts.append(jnp.where(inside, moved, jnp.zeros_like(moved)))
    groups = round_up(ks * image.shape[0], LANES) // image.shape[0]
    parts += [jnp.zeros_like(image)] * (groups - ks)
    return jnp.concatenate(parts, axis=0)


def spatial_kernel(*refs):
    more = (len(refs) - 9) // 2
    rad_hbm, taps_hbm = refs[:2]
    far = refs[2:2 + more]
    out_ref, cols_ref = refs[2 + more:4 + more]
    kept = refs[4 + more:4 + 2 * more]
    rad_ref, taps_ref, spread_ref, rows_ref, sems = refs[4 + 2 * more:]
    bands, rows, _ = rad_ref.shape
    chunk = bands // LOADS
    taps_copy = pltpu.make_async_copy(taps_hbm, taps_ref, sems.at[LOADS])
    taps_copy.start()
    loads = []
    for k in range(LOADS):
        part = pl.ds(k * chunk, chunk)
        loads.append(pltpu.make_async_copy(rad_hbm.at[part], rad_ref.at[part], sems.at[k]))
        loads[-1].start()
    others = []
    for k in range(more):
        others.append(pltpu.make_async_copy(far[k], kept[k], sems.at[LOADS + 1 + k]))
        others[-1].start()
    ks = taps_ref.shape[0]
    half = ks // 2
    per = LANES // rows
    tiles = spread_ref.shape[1] // LANES
    lane, row = lane_row((ks, tiles * LANES))
    taps_copy.wait()
    spread = jnp.zeros((bands, tiles * LANES), F32)
    for i in range(ks):
        home = (row // per) * LANES + ((row % per) * rows + (i - half) + LANES) % LANES
        hot = (lane == home).astype(BF16)
        spread += lax.dot_general(taps_ref[i], hot, (((0,), (0,)), ((), ())), preferred_element_type=F32)
    spread_ref[...] = spread
    keep = near_diagonal(rows, half)
    for b in range(bands):
        if b % chunk == 0:
            loads[b // chunk].wait()
        columns = shifted_columns(rad_ref[b], ks)
        cols_ref[b] = columns
        mats = []
        for t in range(tiles):
            line = spread_ref[b:b + 1, t * LANES:(t + 1) * LANES]
            wide = jnp.broadcast_to(line, (rows, LANES))
            wide = pltpu.roll(wide, 0, 1, stride=1, stride_axis=0)
            mats.append(jnp.where(keep, wide, 0.0))
        mix = jnp.concatenate(mats, axis=1).astype(BF16)
        out = jnp.dot(mix, columns, preferred_element_type=F32)
        rows_ref[pl.ds(b, rows, stride=bands), :] = out
    peers, size, _ = out_ref.shape
    count = rows * bands // peers
    for d in range(peers):
        out_ref[d, 0:count, :] = rows_ref[d * count:(d + 1) * count, :].astype(BF16)
        if size > count:
            out_ref[d, count:size, :] = jnp.zeros((size - count, LANES), BF16)
    for copy in others:
        copy.wait()


def net_kernel(spec_ref, first_ref, mid_ref, outer_ref, want_ref, valid_ref, out_ref, a_ref, b_ref, g_ref, *, scale):
    peers, size, _ = spec_ref.shape
    ch, total = first_ref.shape
    rows = valid_ref.shape[0]
    bands = total // peers
    first = first_ref[...]
    middle = mid_ref[...]
    outer = outer_ref[...]
    a_ref[0:rows * total, :] = want_ref[...].astype(F32)
    wanted = jnp.concatenate([a_ref[pl.ds(r, total, stride=rows), :] for r in range(rows)], axis=1)
    for s in range(peers):
        a_ref[s * size:(s + 1) * size, :] = spec_ref[s].astype(F32)
    for s in range(peers):
        for r in range(rows):
            src = s * size + r * bands
            dst = r * total + s * bands
            b_ref[dst:dst + bands, :] = a_ref[src:src + bands, :]
    spectra = jnp.concatenate([b_ref[r * total:(r + 1) * total, :].astype(BF16) for r in range(rows)], axis=1)

    def mm(x, y, dx, dy):
        return lax.dot_general(x, y, (((dx,), (dy,)), ((), ())), preferred_element_type=F32)

    z_first = mm(first, spectra, 1, 0)
    sig_first = jax.nn.sigmoid(z_first)
    hid_first = (z_first * sig_first).astype(BF16)
    z_mid = mm(middle, hid_first, 0, 0)
    sig_mid = jax.nn.sigmoid(z_mid)
    hid_mid = (hid_first.astype(F32) + z_mid * sig_mid).astype(BF16)
    predicted = mm(outer, hid_mid, 0, 0)
    valid = jnp.concatenate([valid_ref[r:r + 1, :] for r in range(rows)], axis=1).astype(F32)
    err = (2.0 * scale * valid * (predicted - wanted)).astype(BF16)
    d_mid = mm(outer, err, 1, 0)
    dz_mid = (d_mid * silu_slope(z_mid, sig_mid)).astype(BF16)
    d_first = d_mid + mm(middle, dz_mid, 1, 0)
    dz_first = (d_first * silu_slope(z_first, sig_first)).astype(BF16)
    slope = mm(first, dz_first, 0, 0)
    for r in range(rows):
        b_ref[r * total:(r + 1) * total, :] = slope[:, r * LANES:(r + 1) * LANES]
    for s in range(peers):
        for r in range(rows):
            src = r * total + s * bands
            dst = s * size + (rows - 1 - r) * bands
            a_ref[dst:dst + bands, :] = b_ref[src:src + bands, :]
    used = rows * bands
    for s in range(peers):
        if size > used:
            a_ref[s * size + used:(s + 1) * size, :] = jnp.zeros((size - used, LANES), F32)
        out_ref[s, 0:size, :] = a_ref[s * size:(s + 1) * size, :].astype(BF16)
    wide = g_ref.shape[1]
    used = 2 * total + ch
    g_ref[:, 0:total] = mm(dz_first, spectra, 1, 1)
    g_ref[:, total:2 * total] = mm(hid_mid, err, 1, 1)
    g_ref[:, 2 * total:used] = mm(hid_first, dz_mid, 1, 1)
    if wide > used:
        g_ref[:, used:wide] = jnp.zeros((ch, wide - used), F32)
    share = ch // peers
    tiles = wide // LANES
    for s in range(peers):
        piece = jnp.concatenate(
            [g_ref[s * share:(s + 1) * share, t * LANES:(t + 1) * LANES] for t in range(tiles)], axis=0
        )
        high = piece.astype(BF16)
        low = (piece - high.astype(F32)).astype(BF16)
        n = tiles * share
        out_ref[s, size:size + n, :] = high
        out_ref[s, size + n:size + 2 * n, :] = low


def kernel_grad_kernel(cols_ref, in_ref, out_ref, rows_ref, acc_ref, *, ks, size):
    bands = cols_ref.shape[0]
    rows = rows_ref.shape[0] // bands
    peers = in_ref.shape[0]
    half = ks // 2
    count = rows * bands // peers
    n = (in_ref.shape[1] - size) // 2
    total = jnp.zeros((n, LANES), F32)
    for s in range(peers):
        total += in_ref[s, size:size + n, :].astype(F32) + in_ref[s, size + n:size + 2 * n, :].astype(F32)
    out_ref[0:n, :] = total
    for s in range(peers):
        back = peers - 1 - s
        rows_ref[back * count:(back + 1) * count, :] = in_ref[s, 0:size, :].astype(F32)[0:count]
    keep = near_diagonal(rows, half, upside_down=True)
    per = LANES // rows
    tiles = -(-ks // per)
    for b in range(bands):
        slope = rows_ref[pl.ds(b, rows, stride=bands), :].astype(BF16)
        full = lax.dot_general(slope, cols_ref[b], (((1,), (1,)), ((), ())), preferred_element_type=F32)
        acc = jnp.zeros((8, LANES), F32)
        for t in range(tiles):
            part = jnp.where(keep, full[:, t * LANES:(t + 1) * LANES], 0.0)
            part = pltpu.roll(part, LANES + 1 - rows, 1, stride=1, stride_axis=0)
            part = jnp.sum(part.reshape(rows // 8, 8, LANES), axis=0)
            if t:
                part = pltpu.roll(part, t * (ks + 1), 1)
            acc += part
        acc_ref[b * 8:(b + 1) * 8, :] = acc
    result = acc_ref[pl.ds(0, bands, stride=8), :]
    for k in range(1, 8):
        result += acc_ref[pl.ds(k, bands, stride=8), :]
    out_ref[n:n + bands, :] = result
    rest = out_ref.shape[0] - n - bands
    if rest:
        out_ref[n + bands:n + bands + rest, :] = jnp.zeros((rest, LANES), F32)


def join_kernel(a_ref, b_ref, c_ref, d_ref, all_ref, own_ref):
    value = (a_ref[...] + b_ref[...]) + (c_ref[...] + d_ref[...])
    peers, n, _ = all_ref.shape
    for s in range(peers):
        all_ref[s] = value[0:n]
    own_ref[...] = value[n:]


def final_kernel(all_ref, own_ref, gk_ref, gf_ref, gm_ref, go_ref, t_ref, g_ref, *, rows):
    ks, _, bands = gk_ref.shape
    half = ks // 2
    per = LANES // rows
    t_ref[...] = own_ref[...].T
    for i in range(ks):
        for j in range(ks):
            lane = ((j % per) * rows + (j // per) * (ks + 1) + (i - half)) % LANES
            gk_ref[i, j:j + 1, :] = t_ref[lane:lane + 1, 0:bands]
    peers, n, _ = all_ref.shape
    ch, total = gf_ref.shape
    share = ch // peers
    for s in range(peers):
        for t in range(n // share):
            g_ref[s * share:(s + 1) * share, t * LANES:(t + 1) * LANES] = all_ref[s, t * share:(t + 1) * share, :]
    gf_ref[...] = g_ref[:, 0:total]
    go_ref[...] = g_ref[:, total:2 * total]
    gm_ref[...] = g_ref[:, 2 * total:2 * total + ch]


def near(*arrays):
    return [pltpu.with_memory_space_constraint(a, pltpu.VMEM) for a in arrays]


def spots(count):
    return [pl.BlockSpec(memory_space=pltpu.VMEM)] * count


def exchange(block, axis):
    return lax.all_to_all(block, axis, split_axis=0, concat_axis=0, tiled=True)


def group_parts(value, axis, stride):
    members = lax.axis_size(axis)

    def other(flip):
        return lax.ppermute(value, axis, [(i, i ^ flip) for i in range(members)])

    return (value, other(stride), other(2 * stride), other(3 * stride))


def on_device(radiance, kernel, w_first, w_mid, w_out, target, mask):
    image = radiance[0]
    bands, rows_all, width = image.shape
    ks = kernel.shape[1]
    peers = lax.axis_size("band")
    crops = lax.axis_size("dp")
    rows = mask.shape[1]
    total, ch = w_first.shape
    scale = 1.0 / math.sqrt(crops * rows_all * width)
    size = round_up(rows * bands, 16)
    taps = jnp.transpose(kernel, (1, 2, 0))
    first = jnp.transpose(w_first, (1, 0))
    wanted = target[0].reshape(total * rows, width)
    spread_wide = round_up(ks * rows_all, LANES)
    params = (image, taps, first, w_mid, w_out, wanted, mask[0])
    filtered, columns, first, w_mid, w_out, wanted, valid = pl.pallas_call(
        spatial_kernel,
        in_specs=[pl.BlockSpec(memory_space=pltpu.HBM)] * len(params),
        out_specs=spots(len(params)),
        out_shape=(pltpu.VMEM((peers, size, width), BF16), pltpu.VMEM((bands, spread_wide, width), BF16))
        + tuple(pltpu.VMEM(p.shape, p.dtype) for p in params[2:]),
        scratch_shapes=[
            pltpu.VMEM(image.shape, BF16),
            pltpu.VMEM(taps.shape, BF16),
            pltpu.VMEM((bands, spread_wide), F32),
            pltpu.VMEM((bands * rows_all, width), F32),
            pltpu.SemaphoreType.DMA((LOADS + len(params),)),
        ],
        compiler_params=SMALL,
        name="spatial",
    )(*[pltpu.with_memory_space_constraint(p, pltpu.HBM) for p in params])
    spectra = exchange(filtered, "band")
    wide = round_up(2 * total + ch, LANES)
    share_rows = wide // LANES * (ch // peers)
    packed = pl.pallas_call(
        functools.partial(net_kernel, scale=scale),
        in_specs=spots(6),
        out_specs=spots(1)[0],
        out_shape=pltpu.VMEM((peers, size + 2 * share_rows, width), BF16),
        scratch_shapes=[
            pltpu.VMEM((peers * size, width), F32),
            pltpu.VMEM((rows * total, width), F32),
            pltpu.VMEM((ch, wide), F32),
        ],
        compiler_params=SMALL,
        name="net",
    )(*near(spectra, first, w_mid, w_out, wanted, valid))
    packed = exchange(packed, "band")
    bands_up = round_up(bands, 8)
    sums = pl.pallas_call(
        functools.partial(kernel_grad_kernel, ks=ks, size=size),
        in_specs=spots(2),
        out_specs=spots(1)[0],
        out_shape=pltpu.VMEM((share_rows + bands_up, width), F32),
        scratch_shapes=[pltpu.VMEM((bands * rows_all, width), F32), pltpu.VMEM((bands * 8, width), F32)],
        compiler_params=SMALL,
        name="kernel_grad",
    )(*near(columns, packed))
    sums = sums + lax.ppermute(sums, "dp", [(i, i ^ 1) for i in range(crops)])
    if crops == 32:
        a, b, c, d = group_parts(sums, "dp", 2)
        sums = (a + b) + (c + d)
        parts = group_parts(sums, "dp", 8)
    else:
        parts = (sums,) + (jnp.zeros_like(sums),) * 3
    shared, own = pl.pallas_call(
        join_kernel,
        in_specs=spots(4),
        out_specs=spots(2),
        out_shape=(pltpu.VMEM((peers, share_rows, width), F32), pltpu.VMEM((bands_up, width), F32)),
        compiler_params=SMALL,
        name="join",
    )(*near(*parts))
    shared = exchange(shared, "band")
    grad_kernel, grad_first, grad_mid, grad_out = pl.pallas_call(
        functools.partial(final_kernel, rows=rows_all),
        in_specs=spots(2),
        out_shape=(
            jax.ShapeDtypeStruct((ks, ks, bands), F32),
            jax.ShapeDtypeStruct((ch, total), F32),
            jax.ShapeDtypeStruct((ch, ch), F32),
            jax.ShapeDtypeStruct((ch, total), F32),
        ),
        scratch_shapes=[pltpu.VMEM((LANES, bands_up), F32), pltpu.VMEM((ch, wide), F32)],
        compiler_params=SMALL,
        name="final",
    )(*near(shared, own))
    return (jnp.transpose(grad_kernel, (2, 0, 1)), jnp.transpose(grad_first, (1, 0)), grad_mid, grad_out)


def solution(mesh):
    in_specs = (
        P("dp", "band", None, None),
        P("band", None, None),
        P(),
        P(),
        P(),
        P("dp", None, "band", None),
        P("dp", "band", None),
    )
    out_specs = (P("band", None, None), P(), P(), P())
    return jax.shard_map(on_device, mesh=mesh, in_specs=in_specs, out_specs=out_specs, check_vma=False)
```

```python
import functools
import math

import jax
import jax.numpy as jnp
from jax import lax
from jax.experimental import pallas as pl
from jax.experimental.pallas import tpu as pltpu
from jax.sharding import PartitionSpec as P

F32 = jnp.float32
BF16 = jnp.bfloat16
LANES = 128
LOADS = 1
SMALL = pltpu.CompilerParams(vmem_limit_bytes=16 << 20)


def round_up(value, step):
    return -(-value // step) * step


def silu_slope(value, sig):
    return sig * (1.0 + value * (1.0 - sig))


def lane_row(shape):
    return (lax.broadcasted_iota(jnp.int32, shape, 1), lax.broadcasted_iota(jnp.int32, shape, 0))


def near_diagonal(rows, half, upside_down=False):
    lane, row = lane_row((rows, LANES))
    if upside_down:
        row = rows - 1 - row
    away = lane % rows - row
    return (away >= -half) & (away <= half)


def shifted_columns(image, ks):
    half = ks // 2
    lane, _ = lane_row(image.shape)
    parts = []
    for j in range(ks):
        step = j - half
        if step == 0:
            parts.append(image)
            continue
        moved = pltpu.roll(image, (-step) % LANES, 1)
        inside = lane < LANES - step if step > 0 else lane >= -step
        parts.append(jnp.where(inside, moved, jnp.zeros_like(moved)))
    groups = round_up(ks * image.shape[0], LANES) // image.shape[0]
    parts += [jnp.zeros_like(image)] * (groups - ks)
    return jnp.concatenate(parts, axis=0)


def spatial_kernel(*refs):
    more = (len(refs) - 9) // 2
    rad_hbm, taps_hbm = refs[:2]
    far = refs[2:2 + more]
    out_ref, cols_ref = refs[2 + more:4 + more]
    kept = refs[4 + more:4 + 2 * more]
    rad_ref, taps_ref, spread_ref, rows_ref, sems = refs[4 + 2 * more:]
    bands, rows, _ = rad_ref.shape
    chunk = bands // LOADS
    taps_copy = pltpu.make_async_copy(taps_hbm, taps_ref, sems.at[LOADS])
    taps_copy.start()
    loads = []
    for k in range(LOADS):
        part = pl.ds(k * chunk, chunk)
        loads.append(pltpu.make_async_copy(rad_hbm.at[part], rad_ref.at[part], sems.at[k]))
        loads[-1].start()
    others = []
    for k in range(more):
        others.append(pltpu.make_async_copy(far[k], kept[k], sems.at[LOADS + 1 + k]))
        others[-1].start()
    ks = taps_ref.shape[0]
    half = ks // 2
    per = LANES // rows
    tiles = spread_ref.shape[1] // LANES
    lane, row = lane_row((ks, tiles * LANES))
    taps_copy.wait()
    spread = jnp.zeros((bands, tiles * LANES), F32)
    for i in range(ks):
        home = (row // per) * LANES + ((row % per) * rows + (i - half) + LANES) % LANES
        hot = (lane == home).astype(BF16)
        spread += lax.dot_general(taps_ref[i], hot, (((0,), (0,)), ((), ())), preferred_element_type=F32)
    spread_ref[...] = spread
    keep = near_diagonal(rows, half)
    for b in range(bands):
        if b % chunk == 0:
            loads[b // chunk].wait()
        columns = shifted_columns(rad_ref[b], ks)
        cols_ref[b] = columns
        mats = []
        for t in range(tiles):
            line = spread_ref[b:b + 1, t * LANES:(t + 1) * LANES]
            wide = jnp.broadcast_to(line, (rows, LANES))
            wide = pltpu.roll(wide, 0, 1, stride=1, stride_axis=0)
            mats.append(jnp.where(keep, wide, 0.0))
        mix = jnp.concatenate(mats, axis=1).astype(BF16)
        out = jnp.dot(mix, columns, preferred_element_type=F32)
        rows_ref[pl.ds(b, rows, stride=bands), :] = out
    peers, size, _ = out_ref.shape
    count = rows * bands // peers
    for d in range(peers):
        out_ref[d, 0:count, :] = rows_ref[d * count:(d + 1) * count, :].astype(BF16)
        if size > count:
            out_ref[d, count:size, :] = jnp.zeros((size - count, LANES), BF16)
    for copy in others:
        copy.wait()


def net_kernel(spec_ref, first_ref, mid_ref, outer_ref, want_ref, valid_ref, out_ref, a_ref, b_ref, g_ref, *, scale):
    peers, size, _ = spec_ref.shape
    ch, total = first_ref.shape
    rows = valid_ref.shape[0]
    bands = total // peers
    first = first_ref[...]
    middle = mid_ref[...]
    outer = outer_ref[...]
    a_ref[0:rows * total, :] = want_ref[...].astype(F32)
    wanted = jnp.concatenate([a_ref[pl.ds(r, total, stride=rows), :] for r in range(rows)], axis=1)
    for s in range(peers):
        a_ref[s * size:(s + 1) * size, :] = spec_ref[s].astype(F32)
    for s in range(peers):
        for r in range(rows):
            src = s * size + r * bands
            dst = r * total + s * bands
            b_ref[dst:dst + bands, :] = a_ref[src:src + bands, :]
    spectra = jnp.concatenate([b_ref[r * total:(r + 1) * total, :].astype(BF16) for r in range(rows)], axis=1)

    def mm(x, y, dx, dy):
        return lax.dot_general(x, y, (((dx,), (dy,)), ((), ())), preferred_element_type=F32)

    z_first = mm(first, spectra, 1, 0)
    sig_first = jax.nn.sigmoid(z_first)
    hid_first = (z_first * sig_first).astype(BF16)
    z_mid = mm(middle, hid_first, 0, 0)
    sig_mid = jax.nn.sigmoid(z_mid)
    hid_mid = (hid_first.astype(F32) + z_mid * sig_mid).astype(BF16)
    predicted = mm(outer, hid_mid, 0, 0)
    valid = jnp.concatenate([valid_ref[r:r + 1, :] for r in range(rows)], axis=1).astype(F32)
    err = (2.0 * scale * valid * (predicted - wanted)).astype(BF16)
    d_mid = mm(outer, err, 1, 0)
    dz_mid = (d_mid * silu_slope(z_mid, sig_mid)).astype(BF16)
    d_first = d_mid + mm(middle, dz_mid, 1, 0)
    dz_first = (d_first * silu_slope(z_first, sig_first)).astype(BF16)
    slope = mm(first, dz_first, 0, 0)
    for r in range(rows):
        b_ref[r * total:(r + 1) * total, :] = slope[:, r * LANES:(r + 1) * LANES]
    for s in range(peers):
        for r in range(rows):
            src = r * total + s * bands
            dst = s * size + (rows - 1 - r) * bands
            a_ref[dst:dst + bands, :] = b_ref[src:src + bands, :]
    used = rows * bands
    for s in range(peers):
        if size > used:
            a_ref[s * size + used:(s + 1) * size, :] = jnp.zeros((size - used, LANES), F32)
        out_ref[s, 0:size, :] = a_ref[s * size:(s + 1) * size, :].astype(BF16)
    wide = g_ref.shape[1]
    used = 2 * total + ch
    g_ref[:, 0:total] = mm(dz_first, spectra, 1, 1)
    g_ref[:, total:2 * total] = mm(hid_mid, err, 1, 1)
    g_ref[:, 2 * total:used] = mm(hid_first, dz_mid, 1, 1)
    if wide > used:
        g_ref[:, used:wide] = jnp.zeros((ch, wide - used), F32)
    share = ch // peers
    tiles = wide // LANES
    for s in range(peers):
        piece = jnp.concatenate(
            [g_ref[s * share:(s + 1) * share, t * LANES:(t + 1) * LANES] for t in range(tiles)], axis=0
        )
        high = piece.astype(BF16)
        low = (piece - high.astype(F32)).astype(BF16)
        n = tiles * share
        out_ref[s, size:size + n, :] = high
        out_ref[s, size + n:size + 2 * n, :] = low


def kernel_grad_kernel(cols_ref, in_ref, out_ref, rows_ref, acc_ref, *, ks, size):
    bands = cols_ref.shape[0]
    rows = rows_ref.shape[0] // bands
    peers = in_ref.shape[0]
    half = ks // 2
    count = rows * bands // peers
    n = (in_ref.shape[1] - size) // 2
    total = jnp.zeros((n, LANES), F32)
    for s in range(peers):
        total += in_ref[s, size:size + n, :].astype(F32) + in_ref[s, size + n:size + 2 * n, :].astype(F32)
    out_ref[0:n, :] = total
    for s in range(peers):
        back = peers - 1 - s
        rows_ref[back * count:(back + 1) * count, :] = in_ref[s, 0:size, :].astype(F32)[0:count]
    keep = near_diagonal(rows, half, upside_down=True)
    per = LANES // rows
    tiles = -(-ks // per)
    for b in range(bands):
        slope = rows_ref[pl.ds(b, rows, stride=bands), :].astype(BF16)
        full = lax.dot_general(slope, cols_ref[b], (((1,), (1,)), ((), ())), preferred_element_type=F32)
        acc = jnp.zeros((8, LANES), F32)
        for t in range(tiles):
            part = jnp.where(keep, full[:, t * LANES:(t + 1) * LANES], 0.0)
            part = pltpu.roll(part, LANES + 1 - rows, 1, stride=1, stride_axis=0)
            part = jnp.sum(part.reshape(rows // 8, 8, LANES), axis=0)
            if t:
                part = pltpu.roll(part, t * (ks + 1), 1)
            acc += part
        acc_ref[b * 8:(b + 1) * 8, :] = acc
    near_half = (bands + 1) // 2
    far_half = bands - near_half
    top = acc_ref[pl.ds(0, near_half, stride=8), :]
    bottom = acc_ref[pl.ds(8 * near_half, far_half, stride=8), :]
    for k in range(1, 8):
        top += acc_ref[pl.ds(k, near_half, stride=8), :]
        bottom += acc_ref[pl.ds(8 * near_half + k, far_half, stride=8), :]
    out_ref[n:, :] = jnp.zeros((out_ref.shape[0] - n, LANES), F32)
    out_ref[n:n + near_half, :] = top
    out_ref[n:n + far_half, :] += pltpu.roll(bottom, 2 * (ks + 1), 1)


def join_kernel(a_ref, b_ref, all_ref, own_ref):
    value = a_ref[...] + b_ref[...]
    peers, n, _ = all_ref.shape
    for s in range(peers):
        all_ref[s] = value[0:n]
    own_ref[...] = value[n:]


def final_kernel(all_ref, own_ref, gk_ref, gf_ref, gm_ref, go_ref, t_ref, g_ref, *, rows):
    ks, _, bands = gk_ref.shape
    half = ks // 2
    per = LANES // rows
    near_half = (bands + 1) // 2
    far_half = bands - near_half
    step = 2 * (ks + 1)
    turned = own_ref[...].T
    t_ref[:, 0:near_half] = turned[:, 0:near_half]
    t_ref[0:LANES - step, near_half:bands] = turned[step:LANES, 0:far_half]
    t_ref[LANES - step:LANES, near_half:bands] = turned[0:step, 0:far_half]
    for i in range(ks):
        for j in range(ks):
            lane = ((j % per) * rows + (j // per) * (ks + 1) + (i - half)) % LANES
            gk_ref[i, j:j + 1, :] = t_ref[lane:lane + 1, 0:bands]
    peers, n, _ = all_ref.shape
    ch, total = gf_ref.shape
    share = ch // peers
    for s in range(peers):
        for t in range(n // share):
            g_ref[s * share:(s + 1) * share, t * LANES:(t + 1) * LANES] = all_ref[s, t * share:(t + 1) * share, :]
    gf_ref[...] = g_ref[:, 0:total]
    go_ref[...] = g_ref[:, total:2 * total]
    gm_ref[...] = g_ref[:, 2 * total:2 * total + ch]


def near(*arrays):
    return [pltpu.with_memory_space_constraint(a, pltpu.VMEM) for a in arrays]


def spots(count):
    return [pl.BlockSpec(memory_space=pltpu.VMEM)] * count


def exchange(block, axis):
    return lax.all_to_all(block, axis, split_axis=0, concat_axis=0, tiled=True)


def other(value, axis, flip):
    return lax.ppermute(value, axis, [(i, i ^ flip) for i in range(lax.axis_size(axis))])


def reduce_parts(value, axis):
    members = lax.axis_size(axis)
    value = value + other(value, axis, 1)
    if members >= 8:
        value = (value + other(value, axis, 2)) + (other(value, axis, 4) + other(value, axis, 6))
    if members >= 32:
        value = value + other(value, axis, 8)
        return (value, other(value, axis, 24))
    return (value, jnp.zeros_like(value))


def on_device(radiance, kernel, w_first, w_mid, w_out, target, mask):
    image = radiance[0]
    bands, rows_all, width = image.shape
    ks = kernel.shape[1]
    peers = lax.axis_size("band")
    crops = lax.axis_size("dp")
    rows = mask.shape[1]
    total, ch = w_first.shape
    scale = 1.0 / math.sqrt(crops * rows_all * width)
    size = round_up(rows * bands, 16)
    taps = jnp.transpose(kernel, (1, 2, 0))
    first = jnp.transpose(w_first, (1, 0))
    wanted = target[0].reshape(total * rows, width)
    spread_wide = round_up(ks * rows_all, LANES)
    params = (image, taps, first, w_mid, w_out, wanted, mask[0])
    filtered, columns, first, w_mid, w_out, wanted, valid = pl.pallas_call(
        spatial_kernel,
        in_specs=[pl.BlockSpec(memory_space=pltpu.HBM)] * len(params),
        out_specs=spots(len(params)),
        out_shape=(pltpu.VMEM((peers, size, width), BF16), pltpu.VMEM((bands, spread_wide, width), BF16))
        + tuple(pltpu.VMEM(p.shape, p.dtype) for p in params[2:]),
        scratch_shapes=[
            pltpu.VMEM(image.shape, BF16),
            pltpu.VMEM(taps.shape, BF16),
            pltpu.VMEM((bands, spread_wide), F32),
            pltpu.VMEM((bands * rows_all, width), F32),
            pltpu.SemaphoreType.DMA((LOADS + len(params),)),
        ],
        compiler_params=SMALL,
        name="spatial",
    )(*[pltpu.with_memory_space_constraint(p, pltpu.HBM) for p in params])
    spectra = exchange(filtered, "band")
    wide = round_up(2 * total + ch, LANES)
    share_rows = wide // LANES * (ch // peers)
    packed = pl.pallas_call(
        functools.partial(net_kernel, scale=scale),
        in_specs=spots(6),
        out_specs=spots(1)[0],
        out_shape=pltpu.VMEM((peers, size + 2 * share_rows, width), BF16),
        scratch_shapes=[
            pltpu.VMEM((peers * size, width), F32),
            pltpu.VMEM((rows * total, width), F32),
            pltpu.VMEM((ch, wide), F32),
        ],
        compiler_params=SMALL,
        name="net",
    )(*near(spectra, first, w_mid, w_out, wanted, valid))
    packed = exchange(packed, "band")
    half_up = round_up((bands + 1) // 2, 8)
    sums = pl.pallas_call(
        functools.partial(kernel_grad_kernel, ks=ks, size=size),
        in_specs=spots(2),
        out_specs=spots(1)[0],
        out_shape=pltpu.VMEM((share_rows + half_up, width), F32),
        scratch_shapes=[pltpu.VMEM((bands * rows_all, width), F32), pltpu.VMEM((bands * 8, width), F32)],
        compiler_params=SMALL,
        name="kernel_grad",
    )(*near(columns, packed))
    parts = reduce_parts(sums, "dp")
    shared, own = pl.pallas_call(
        join_kernel,
        in_specs=spots(2),
        out_specs=spots(2),
        out_shape=(pltpu.VMEM((peers, share_rows, width), F32), pltpu.VMEM((half_up, width), F32)),
        compiler_params=SMALL,
        name="join",
    )(*near(*parts))
    shared = exchange(shared, "band")
    grad_kernel, grad_first, grad_mid, grad_out = pl.pallas_call(
        functools.partial(final_kernel, rows=rows_all),
        in_specs=spots(2),
        out_shape=(
            jax.ShapeDtypeStruct((ks, ks, bands), F32),
            jax.ShapeDtypeStruct((ch, total), F32),
            jax.ShapeDtypeStruct((ch, ch), F32),
            jax.ShapeDtypeStruct((ch, total), F32),
        ),
        scratch_shapes=[pltpu.VMEM((LANES, bands), F32), pltpu.VMEM((ch, wide), F32)],
        compiler_params=SMALL,
        name="final",
    )(*near(shared, own))
    return (jnp.transpose(grad_kernel, (2, 0, 1)), jnp.transpose(grad_first, (1, 0)), grad_mid, grad_out)


def solution(mesh):
    in_specs = (
        P("dp", "band", None, None),
        P("band", None, None),
        P(),
        P(),
        P(),
        P("dp", None, "band", None),
        P("dp", "band", None),
    )
    out_specs = (P("band", None, None), P(), P(), P())
    return jax.shard_map(on_device, mesh=mesh, in_specs=in_specs, out_specs=out_specs, check_vma=False)
```

```python
import functools
import math

import jax
import jax.numpy as jnp
from jax import lax
from jax.experimental import pallas as pl
from jax.experimental.pallas import tpu as pltpu
from jax.sharding import PartitionSpec as P

F32 = jnp.float32
BF16 = jnp.bfloat16
LANES = 128
LOADS = 1
SMALL = pltpu.CompilerParams(vmem_limit_bytes=16 << 20)


def round_up(value, step):
    return -(-value // step) * step


def silu_slope(value, sig):
    return sig * (1.0 + value * (1.0 - sig))


def lane_row(shape):
    return (lax.broadcasted_iota(jnp.int32, shape, 1), lax.broadcasted_iota(jnp.int32, shape, 0))


def near_diagonal(rows, half, upside_down=False):
    lane, row = lane_row((rows, LANES))
    if upside_down:
        row = rows - 1 - row
    away = lane % rows - row
    return (away >= -half) & (away <= half)


def shifted_columns(image, ks):
    half = ks // 2
    lane, _ = lane_row(image.shape)
    parts = []
    for j in range(ks):
        step = j - half
        if step == 0:
            parts.append(image)
            continue
        moved = pltpu.roll(image, (-step) % LANES, 1)
        inside = lane < LANES - step if step > 0 else lane >= -step
        parts.append(jnp.where(inside, moved, jnp.zeros_like(moved)))
    groups = round_up(ks * image.shape[0], LANES) // image.shape[0]
    parts += [jnp.zeros_like(image)] * (groups - ks)
    return jnp.concatenate(parts, axis=0)


def spatial_kernel(*refs):
    more = (len(refs) - 9) // 2
    rad_hbm, taps_hbm = refs[:2]
    far = refs[2:2 + more]
    out_ref, cols_ref = refs[2 + more:4 + more]
    kept = refs[4 + more:4 + 2 * more]
    rad_ref, taps_ref, spread_ref, rows_ref, sems = refs[4 + 2 * more:]
    bands, rows, _ = rad_ref.shape
    chunk = bands // LOADS
    taps_copy = pltpu.make_async_copy(taps_hbm, taps_ref, sems.at[LOADS])
    taps_copy.start()
    loads = []
    for k in range(LOADS):
        part = pl.ds(k * chunk, chunk)
        loads.append(pltpu.make_async_copy(rad_hbm.at[part], rad_ref.at[part], sems.at[k]))
        loads[-1].start()
    others = []
    for k in range(more):
        others.append(pltpu.make_async_copy(far[k], kept[k], sems.at[LOADS + 1 + k]))
        others[-1].start()
    ks = taps_ref.shape[0]
    half = ks // 2
    per = LANES // rows
    tiles = spread_ref.shape[1] // LANES
    lane, row = lane_row((ks, tiles * LANES))
    taps_copy.wait()
    spread = jnp.zeros((bands, tiles * LANES), F32)
    for i in range(ks):
        home = (row // per) * LANES + ((row % per) * rows + (i - half) + LANES) % LANES
        hot = (lane == home).astype(BF16)
        spread += lax.dot_general(taps_ref[i], hot, (((0,), (0,)), ((), ())), preferred_element_type=F32)
    spread_ref[...] = spread
    keep = near_diagonal(rows, half)
    for b in range(bands):
        if b % chunk == 0:
            loads[b // chunk].wait()
        columns = shifted_columns(rad_ref[b], ks)
        cols_ref[b] = columns
        mats = []
        for t in range(tiles):
            line = spread_ref[b:b + 1, t * LANES:(t + 1) * LANES]
            wide = jnp.broadcast_to(line, (rows, LANES))
            wide = pltpu.roll(wide, 0, 1, stride=1, stride_axis=0)
            mats.append(jnp.where(keep, wide, 0.0))
        mix = jnp.concatenate(mats, axis=1).astype(BF16)
        out = jnp.dot(mix, columns, preferred_element_type=F32)
        rows_ref[pl.ds(b, rows, stride=bands), :] = out
    peers, size, _ = out_ref.shape
    count = rows * bands // peers
    for d in range(peers):
        out_ref[d, 0:count, :] = rows_ref[d * count:(d + 1) * count, :].astype(BF16)
        if size > count:
            out_ref[d, count:size, :] = jnp.zeros((size - count, LANES), BF16)
    for copy in others:
        copy.wait()


def net_kernel(spec_ref, first_ref, mid_ref, outer_ref, want_ref, valid_ref, out_ref, a_ref, b_ref, g_ref, w_ref, *, scale):
    peers, size, _ = spec_ref.shape
    ch, total = first_ref.shape
    rows = valid_ref.shape[0]
    bands = total // peers
    first = first_ref[...]
    middle = mid_ref[...]
    outer = outer_ref[...]
    for s in range(peers):
        a_ref[s * size:(s + 1) * size, :] = spec_ref[s].astype(F32)
    for s in range(peers):
        for r in range(rows):
            src = s * size + r * bands
            dst = r * total + s * bands
            b_ref[dst:dst + bands, :] = a_ref[src:src + bands, :]
    spectra = jnp.concatenate([b_ref[r * total:(r + 1) * total, :].astype(BF16) for r in range(rows)], axis=1)

    def mm(x, y, dx, dy):
        return lax.dot_general(x, y, (((dx,), (dy,)), ((), ())), preferred_element_type=F32)

    z_first = mm(first, spectra, 1, 0)
    sig_first = jax.nn.sigmoid(z_first)
    hid_first = (z_first * sig_first).astype(BF16)
    z_mid = mm(middle, hid_first, 0, 0)
    sig_mid = jax.nn.sigmoid(z_mid)
    hid_mid = (hid_first.astype(F32) + z_mid * sig_mid).astype(BF16)
    predicted = mm(outer, hid_mid, 0, 0)
    valid = jnp.concatenate([valid_ref[r:r + 1, :] for r in range(rows)], axis=1).astype(F32)
    w_ref[...] = want_ref[...].astype(F32)
    wanted = jnp.concatenate([w_ref[pl.ds(r, total, stride=rows), :] for r in range(rows)], axis=1)
    err = (2.0 * scale * valid * (predicted - wanted)).astype(BF16)
    wide = g_ref.shape[1]
    grads = 2 * total + ch
    d_mid = mm(outer, err, 1, 0)
    g_ref[:, total:2 * total] = mm(hid_mid, err, 1, 1)
    dz_mid = (d_mid * silu_slope(z_mid, sig_mid)).astype(BF16)
    d_first = d_mid + mm(middle, dz_mid, 1, 0)
    g_ref[:, 2 * total:grads] = mm(hid_first, dz_mid, 1, 1)
    if wide > grads:
        g_ref[:, grads:wide] = jnp.zeros((ch, wide - grads), F32)
    dz_first = (d_first * silu_slope(z_first, sig_first)).astype(BF16)
    g_ref[:, 0:total] = mm(dz_first, spectra, 1, 1)
    slope = mm(first, dz_first, 0, 0)
    for r in range(rows):
        b_ref[r * total:(r + 1) * total, :] = slope[:, r * LANES:(r + 1) * LANES]
    for s in range(peers):
        for r in range(rows):
            src = r * total + s * bands
            dst = s * size + (rows - 1 - r) * bands
            a_ref[dst:dst + bands, :] = b_ref[src:src + bands, :]
    used = rows * bands
    for s in range(peers):
        if size > used:
            a_ref[s * size + used:(s + 1) * size, :] = jnp.zeros((size - used, LANES), F32)
        out_ref[s, 0:size, :] = a_ref[s * size:(s + 1) * size, :].astype(BF16)
    share = ch // peers
    tiles = wide // LANES
    for s in range(peers):
        piece = jnp.concatenate(
            [g_ref[s * share:(s + 1) * share, t * LANES:(t + 1) * LANES] for t in range(tiles)], axis=0
        )
        high = piece.astype(BF16)
        low = (piece - high.astype(F32)).astype(BF16)
        n = tiles * share
        out_ref[s, size:size + n, :] = high
        out_ref[s, size + n:size + 2 * n, :] = low


def kernel_grad_kernel(cols_ref, in_ref, out_ref, rows_ref, acc_ref, *, ks, size):
    bands = cols_ref.shape[0]
    rows = rows_ref.shape[0] // bands
    peers = in_ref.shape[0]
    half = ks // 2
    count = rows * bands // peers
    n = (in_ref.shape[1] - size) // 2
    total = jnp.zeros((n, LANES), F32)
    for s in range(peers):
        total += in_ref[s, size:size + n, :].astype(F32) + in_ref[s, size + n:size + 2 * n, :].astype(F32)
    out_ref[0:n, :] = total
    for s in range(peers):
        back = peers - 1 - s
        rows_ref[back * count:(back + 1) * count, :] = in_ref[s, 0:size, :].astype(F32)[0:count]
    keep = near_diagonal(rows, half, upside_down=True)
    per = LANES // rows
    tiles = -(-ks // per)
    for b in range(bands):
        slope = rows_ref[pl.ds(b, rows, stride=bands), :].astype(BF16)
        full = lax.dot_general(slope, cols_ref[b], (((1,), (1,)), ((), ())), preferred_element_type=F32)
        acc = jnp.zeros((8, LANES), F32)
        for t in range(tiles):
            part = jnp.where(keep, full[:, t * LANES:(t + 1) * LANES], 0.0)
            part = pltpu.roll(part, LANES + 1 - rows, 1, stride=1, stride_axis=0)
            part = jnp.sum(part.reshape(rows // 8, 8, LANES), axis=0)
            if t:
                part = pltpu.roll(part, t * (ks + 1), 1)
            acc += part
        acc_ref[b * 8:(b + 1) * 8, :] = acc
    near_half = (bands + 1) // 2
    far_half = bands - near_half
    top = acc_ref[pl.ds(0, near_half, stride=8), :]
    bottom = acc_ref[pl.ds(8 * near_half, far_half, stride=8), :]
    for k in range(1, 8):
        top += acc_ref[pl.ds(k, near_half, stride=8), :]
        bottom += acc_ref[pl.ds(8 * near_half + k, far_half, stride=8), :]
    out_ref[n:, :] = jnp.zeros((out_ref.shape[0] - n, LANES), F32)
    out_ref[n:n + near_half, :] = top
    out_ref[n:n + far_half, :] += pltpu.roll(bottom, 2 * (ks + 1), 1)


def join_kernel(a_ref, b_ref, all_ref, own_ref):
    value = a_ref[...] + b_ref[...]
    peers, n, _ = all_ref.shape
    for s in range(peers):
        all_ref[s] = value[0:n]
    own_ref[...] = value[n:]


def final_kernel(all_ref, own_ref, gk_ref, gf_ref, gm_ref, go_ref, t_ref, g_ref, *, rows):
    ks, _, bands = gk_ref.shape
    half = ks // 2
    per = LANES // rows
    near_half = (bands + 1) // 2
    far_half = bands - near_half
    step = 2 * (ks + 1)
    turned = own_ref[...].T
    t_ref[:, 0:near_half] = turned[:, 0:near_half]
    t_ref[0:LANES - step, near_half:bands] = turned[step:LANES, 0:far_half]
    t_ref[LANES - step:LANES, near_half:bands] = turned[0:step, 0:far_half]
    for i in range(ks):
        for j in range(ks):
            lane = ((j % per) * rows + (j // per) * (ks + 1) + (i - half)) % LANES
            gk_ref[i, j:j + 1, :] = t_ref[lane:lane + 1, 0:bands]
    peers, n, _ = all_ref.shape
    ch, total = gf_ref.shape
    share = ch // peers
    for s in range(peers):
        for t in range(n // share):
            g_ref[s * share:(s + 1) * share, t * LANES:(t + 1) * LANES] = all_ref[s, t * share:(t + 1) * share, :]
    gf_ref[...] = g_ref[:, 0:total]
    go_ref[...] = g_ref[:, total:2 * total]
    gm_ref[...] = g_ref[:, 2 * total:2 * total + ch]


def near(*arrays):
    return [pltpu.with_memory_space_constraint(a, pltpu.VMEM) for a in arrays]


def spots(count):
    return [pl.BlockSpec(memory_space=pltpu.VMEM)] * count


def exchange(block, axis):
    return lax.all_to_all(block, axis, split_axis=0, concat_axis=0, tiled=True)


def other(value, axis, flip):
    return lax.ppermute(value, axis, [(i, i ^ flip) for i in range(lax.axis_size(axis))])


def reduce_parts(value, axis):
    members = lax.axis_size(axis)
    value = value + other(value, axis, 1)
    if members >= 8:
        value = (value + other(value, axis, 2)) + (other(value, axis, 4) + other(value, axis, 6))
    if members >= 32:
        value = value + other(value, axis, 8)
        return (value, other(value, axis, 24))
    return (value, jnp.zeros_like(value))


def on_device(radiance, kernel, w_first, w_mid, w_out, target, mask):
    image = radiance[0]
    bands, rows_all, width = image.shape
    ks = kernel.shape[1]
    peers = lax.axis_size("band")
    crops = lax.axis_size("dp")
    rows = mask.shape[1]
    total, ch = w_first.shape
    scale = 1.0 / math.sqrt(crops * rows_all * width)
    size = round_up(rows * bands, 16)
    taps = jnp.transpose(kernel, (1, 2, 0))
    first = jnp.transpose(w_first, (1, 0))
    wanted = target[0].reshape(total * rows, width)
    spread_wide = round_up(ks * rows_all, LANES)
    params = (image, taps, first, w_mid, w_out, wanted, mask[0])
    filtered, columns, first, w_mid, w_out, wanted, valid = pl.pallas_call(
        spatial_kernel,
        in_specs=[pl.BlockSpec(memory_space=pltpu.HBM)] * len(params),
        out_specs=spots(len(params)),
        out_shape=(pltpu.VMEM((peers, size, width), BF16), pltpu.VMEM((bands, spread_wide, width), BF16))
        + tuple(pltpu.VMEM(p.shape, p.dtype) for p in params[2:]),
        scratch_shapes=[
            pltpu.VMEM(image.shape, BF16),
            pltpu.VMEM(taps.shape, BF16),
            pltpu.VMEM((bands, spread_wide), F32),
            pltpu.VMEM((bands * rows_all, width), F32),
            pltpu.SemaphoreType.DMA((LOADS + len(params),)),
        ],
        compiler_params=SMALL,
        name="spatial",
    )(*[pltpu.with_memory_space_constraint(p, pltpu.HBM) for p in params])
    spectra = exchange(filtered, "band")
    wide = round_up(2 * total + ch, LANES)
    share_rows = wide // LANES * (ch // peers)
    packed = pl.pallas_call(
        functools.partial(net_kernel, scale=scale),
        in_specs=spots(6),
        out_specs=spots(1)[0],
        out_shape=pltpu.VMEM((peers, size + 2 * share_rows, width), BF16),
        scratch_shapes=[
            pltpu.VMEM((peers * size, width), F32),
            pltpu.VMEM((rows * total, width), F32),
            pltpu.VMEM((ch, wide), F32),
            pltpu.VMEM((rows * total, width), F32),
        ],
        compiler_params=SMALL,
        name="net",
    )(*near(spectra, first, w_mid, w_out, wanted, valid))
    packed = exchange(packed, "band")
    half_up = round_up((bands + 1) // 2, 8)
    sums = pl.pallas_call(
        functools.partial(kernel_grad_kernel, ks=ks, size=size),
        in_specs=spots(2),
        out_specs=spots(1)[0],
        out_shape=pltpu.VMEM((share_rows + half_up, width), F32),
        scratch_shapes=[pltpu.VMEM((bands * rows_all, width), F32), pltpu.VMEM((bands * 8, width), F32)],
        compiler_params=SMALL,
        name="kernel_grad",
    )(*near(columns, packed))
    parts = reduce_parts(sums, "dp")
    shared, own = pl.pallas_call(
        join_kernel,
        in_specs=spots(2),
        out_specs=spots(2),
        out_shape=(pltpu.VMEM((peers, share_rows, width), F32), pltpu.VMEM((half_up, width), F32)),
        compiler_params=SMALL,
        name="join",
    )(*near(*parts))
    shared = exchange(shared, "band")
    grad_kernel, grad_first, grad_mid, grad_out = pl.pallas_call(
        functools.partial(final_kernel, rows=rows_all),
        in_specs=spots(2),
        out_shape=(
            jax.ShapeDtypeStruct((ks, ks, bands), F32),
            jax.ShapeDtypeStruct((ch, total), F32),
            jax.ShapeDtypeStruct((ch, ch), F32),
            jax.ShapeDtypeStruct((ch, total), F32),
        ),
        scratch_shapes=[pltpu.VMEM((LANES, bands), F32), pltpu.VMEM((ch, wide), F32)],
        compiler_params=SMALL,
        name="final",
    )(*near(shared, own))
    return (jnp.transpose(grad_kernel, (2, 0, 1)), jnp.transpose(grad_first, (1, 0)), grad_mid, grad_out)


def solution(mesh):
    in_specs = (
        P("dp", "band", None, None),
        P("band", None, None),
        P(),
        P(),
        P(),
        P("dp", None, "band", None),
        P("dp", "band", None),
    )
    out_specs = (P("band", None, None), P(), P(), P())
    return jax.shard_map(on_device, mesh=mesh, in_specs=in_specs, out_specs=out_specs, check_vma=False)
```

```python
import functools
import math

import jax
import jax.numpy as jnp
from jax import lax
from jax.experimental import pallas as pl
from jax.experimental.pallas import tpu as pltpu
from jax.sharding import PartitionSpec as P

F32 = jnp.float32
BF16 = jnp.bfloat16
LANES = 128
LOADS = 1
SMALL = pltpu.CompilerParams(vmem_limit_bytes=16 << 20)


def round_up(value, step):
    return -(-value // step) * step


def silu_slope(value, sig):
    return sig * (1.0 + value * (1.0 - sig))


def lane_row(shape):
    return (lax.broadcasted_iota(jnp.int32, shape, 1), lax.broadcasted_iota(jnp.int32, shape, 0))


def near_diagonal(rows, half, upside_down=False):
    lane, row = lane_row((rows, LANES))
    if upside_down:
        row = rows - 1 - row
    away = lane % rows - row
    return (away >= -half) & (away <= half)


def shifted_columns(image, ks):
    half = ks // 2
    lane, _ = lane_row(image.shape)
    parts = []
    for j in range(ks):
        step = j - half
        if step == 0:
            parts.append(image)
            continue
        moved = pltpu.roll(image, (-step) % LANES, 1)
        inside = lane < LANES - step if step > 0 else lane >= -step
        parts.append(jnp.where(inside, moved, jnp.zeros_like(moved)))
    groups = round_up(ks * image.shape[0], LANES) // image.shape[0]
    parts += [jnp.zeros_like(image)] * (groups - ks)
    return jnp.concatenate(parts, axis=0)


def spatial_kernel(*refs):
    more = (len(refs) - 9) // 2
    rad_hbm, taps_hbm = refs[:2]
    far = refs[2:2 + more]
    out_ref, cols_ref = refs[2 + more:4 + more]
    kept = refs[4 + more:4 + 2 * more]
    rad_ref, taps_ref, spread_ref, rows_ref, sems = refs[4 + 2 * more:]
    bands, rows, _ = rad_ref.shape
    chunk = bands // LOADS
    taps_copy = pltpu.make_async_copy(taps_hbm, taps_ref, sems.at[LOADS])
    taps_copy.start()
    loads = []
    for k in range(LOADS):
        part = pl.ds(k * chunk, chunk)
        loads.append(pltpu.make_async_copy(rad_hbm.at[part], rad_ref.at[part], sems.at[k]))
        loads[-1].start()
    others = []
    for k in range(more):
        others.append(pltpu.make_async_copy(far[k], kept[k], sems.at[LOADS + 1 + k]))
        others[-1].start()
    ks = taps_ref.shape[0]
    half = ks // 2
    per = LANES // rows
    tiles = spread_ref.shape[1] // LANES
    lane, row = lane_row((ks, tiles * LANES))
    taps_copy.wait()
    spread = jnp.zeros((bands, tiles * LANES), F32)
    for i in range(ks):
        home = (row // per) * LANES + ((row % per) * rows + (i - half) + LANES) % LANES
        hot = (lane == home).astype(BF16)
        spread += lax.dot_general(taps_ref[i], hot, (((0,), (0,)), ((), ())), preferred_element_type=F32)
    spread_ref[0:bands, :] = spread
    keep = near_diagonal(rows, half)
    for b in range(bands):
        if b % chunk == 0:
            loads[b // chunk].wait()
        columns = shifted_columns(rad_ref[b], ks)
        cols_ref[b] = columns
        mats = []
        for t in range(tiles):
            line = spread_ref[b:b + 1, t * LANES:(t + 1) * LANES]
            wide = jnp.broadcast_to(line, (rows, LANES))
            wide = pltpu.roll(wide, 0, 1, stride=1, stride_axis=0)
            mats.append(jnp.where(keep, wide, 0.0))
        mix = jnp.concatenate(mats, axis=1).astype(BF16)
        out = jnp.dot(mix, columns, preferred_element_type=F32)
        rows_ref[pl.ds(b, rows, stride=bands), :] = out
    peers, size, _ = out_ref.shape
    count = rows * bands // peers
    for d in range(peers):
        out_ref[d, 0:count, :] = rows_ref[d * count:(d + 1) * count, :].astype(BF16)
        if size > count:
            out_ref[d, count:size, :] = jnp.zeros((size - count, LANES), BF16)
    for copy in others:
        copy.wait()


def net_kernel(spec_ref, first_ref, mid_ref, outer_ref, want_ref, valid_ref, out_ref, a_ref, b_ref, g_ref, w_ref, *, scale):
    peers, size, _ = spec_ref.shape
    ch, total = first_ref.shape
    rows = valid_ref.shape[0]
    bands = total // peers
    first = first_ref[...]
    middle = mid_ref[...]
    outer = outer_ref[...]
    for s in range(peers):
        a_ref[s * size:(s + 1) * size, :] = spec_ref[s].astype(F32)
    for s in range(peers):
        for r in range(rows):
            src = s * size + r * bands
            dst = r * total + s * bands
            b_ref[dst:dst + bands, :] = a_ref[src:src + bands, :]
    spectra = jnp.concatenate([b_ref[r * total:(r + 1) * total, :].astype(BF16) for r in range(rows)], axis=1)

    def mm(x, y, dx, dy):
        return lax.dot_general(x, y, (((dx,), (dy,)), ((), ())), preferred_element_type=F32)

    z_first = mm(first, spectra, 1, 0)
    sig_first = jax.nn.sigmoid(z_first)
    hid_first = (z_first * sig_first).astype(BF16)
    z_mid = mm(middle, hid_first, 0, 0)
    sig_mid = jax.nn.sigmoid(z_mid)
    hid_mid = (hid_first.astype(F32) + z_mid * sig_mid).astype(BF16)
    predicted = mm(outer, hid_mid, 0, 0)
    flags = valid_ref[...].astype(F32)
    valid = jnp.concatenate([flags[r:r + 1, :] for r in range(rows)], axis=1)
    w_ref[...] = want_ref[...].astype(F32)
    wanted = jnp.concatenate([w_ref[pl.ds(r, total, stride=rows), :] for r in range(rows)], axis=1)
    err = (2.0 * scale * valid * (predicted - wanted)).astype(BF16)
    wide = g_ref.shape[1]
    grads = 2 * total + ch
    d_mid = mm(outer, err, 1, 0)
    g_ref[:, total:2 * total] = mm(hid_mid, err, 1, 1)
    dz_mid = (d_mid * silu_slope(z_mid, sig_mid)).astype(BF16)
    d_first = d_mid + mm(middle, dz_mid, 1, 0)
    g_ref[:, 2 * total:grads] = mm(hid_first, dz_mid, 1, 1)
    if wide > grads:
        g_ref[:, grads:wide] = jnp.zeros((ch, wide - grads), F32)
    dz_first = (d_first * silu_slope(z_first, sig_first)).astype(BF16)
    g_ref[:, 0:total] = mm(dz_first, spectra, 1, 1)
    slope = mm(first, dz_first, 0, 0)
    for r in range(rows):
        b_ref[r * total:(r + 1) * total, :] = slope[:, r * LANES:(r + 1) * LANES]
    for s in range(peers):
        for r in range(rows):
            src = r * total + s * bands
            dst = s * size + (rows - 1 - r) * bands
            a_ref[dst:dst + bands, :] = b_ref[src:src + bands, :]
    used = rows * bands
    for s in range(peers):
        if size > used:
            a_ref[s * size + used:(s + 1) * size, :] = jnp.zeros((size - used, LANES), F32)
        out_ref[s, 0:size, :] = a_ref[s * size:(s + 1) * size, :].astype(BF16)
    share = ch // peers
    tiles = wide // LANES
    for s in range(peers):
        piece = jnp.concatenate(
            [g_ref[s * share:(s + 1) * share, t * LANES:(t + 1) * LANES] for t in range(tiles)], axis=0
        )
        high = piece.astype(BF16)
        low = (piece - high.astype(F32)).astype(BF16)
        n = tiles * share
        out_ref[s, size:size + n, :] = high
        out_ref[s, size + n:size + 2 * n, :] = low


def kernel_grad_kernel(cols_ref, in_ref, out_ref, rows_ref, acc_ref, *, ks, rows, size):
    bands = cols_ref.shape[0]
    peers = in_ref.shape[0]
    half = ks // 2
    count = rows * bands // peers
    n = (in_ref.shape[1] - size) // 2
    total = jnp.zeros((n, LANES), F32)
    for s in range(peers):
        total += in_ref[s, size:size + n, :].astype(F32) + in_ref[s, size + n:size + 2 * n, :].astype(F32)
    out_ref[0:n, :] = total
    for s in range(peers):
        back = peers - 1 - s
        rows_ref[back * count:(back + 1) * count, :] = in_ref[s, 0:size, :].astype(F32)[0:count]
    keep = near_diagonal(rows, half, upside_down=True)
    per = LANES // rows
    tiles = -(-ks // per)
    for b in range(bands):
        slope = rows_ref[pl.ds(b, rows, stride=bands), :].astype(BF16)
        full = lax.dot_general(slope, cols_ref[b], (((1,), (1,)), ((), ())), preferred_element_type=F32)
        acc = jnp.zeros((8, LANES), F32)
        for t in range(tiles):
            part = jnp.where(keep, full[:, t * LANES:(t + 1) * LANES], 0.0)
            part = pltpu.roll(part, LANES + 1 - rows, 1, stride=1, stride_axis=0)
            part = jnp.sum(part.reshape(rows // 8, 8, LANES), axis=0)
            if t:
                part = pltpu.roll(part, t * (ks + 1), 1)
            acc += part
        acc_ref[b * 8:(b + 1) * 8, :] = acc
    near_half = (bands + 1) // 2
    far_half = bands - near_half
    top = acc_ref[pl.ds(0, near_half, stride=8), :]
    bottom = acc_ref[pl.ds(8 * near_half, far_half, stride=8), :]
    for k in range(1, 8):
        top += acc_ref[pl.ds(k, near_half, stride=8), :]
        bottom += acc_ref[pl.ds(8 * near_half + k, far_half, stride=8), :]
    out_ref[n:, :] = jnp.zeros((out_ref.shape[0] - n, LANES), F32)
    out_ref[n:n + near_half, :] = top
    out_ref[n:n + far_half, :] += pltpu.roll(bottom, 2 * (ks + 1), 1)


def join_kernel(a_ref, b_ref, all_ref, own_ref):
    value = a_ref[...] + b_ref[...]
    peers, n, _ = all_ref.shape
    for s in range(peers):
        all_ref[s] = value[0:n]
    own_ref[...] = value[n:]


def final_kernel(all_ref, own_ref, gk_ref, gf_ref, gm_ref, go_ref, t_ref, g_ref, *, rows):
    ks, _, bands = gk_ref.shape
    half = ks // 2
    per = LANES // rows
    near_half = (bands + 1) // 2
    far_half = bands - near_half
    step = 2 * (ks + 1)
    turned = own_ref[...].T
    t_ref[0:LANES, 0:near_half] = turned[:, 0:near_half]
    t_ref[0:LANES - step, near_half:bands] = turned[step:LANES, 0:far_half]
    t_ref[LANES - step:LANES, near_half:bands] = turned[0:step, 0:far_half]
    for i in range(ks):
        for j in range(ks):
            lane = ((j % per) * rows + (j // per) * (ks + 1) + (i - half)) % LANES
            gk_ref[i, j:j + 1, :] = t_ref[lane:lane + 1, 0:bands]
    peers, n, _ = all_ref.shape
    ch, total = gf_ref.shape
    share = ch // peers
    for s in range(peers):
        for t in range(n // share):
            g_ref[s * share:(s + 1) * share, t * LANES:(t + 1) * LANES] = all_ref[s, t * share:(t + 1) * share, :]
    gf_ref[...] = g_ref[:, 0:total]
    go_ref[...] = g_ref[:, total:2 * total]
    gm_ref[...] = g_ref[:, 2 * total:2 * total + ch]


def near(*arrays):
    return [pltpu.with_memory_space_constraint(a, pltpu.VMEM) for a in arrays]


def spots(count):
    return [pl.BlockSpec(memory_space=pltpu.VMEM)] * count


def exchange(block, axis):
    return lax.all_to_all(block, axis, split_axis=0, concat_axis=0, tiled=True)


def other(value, axis, flip):
    return lax.ppermute(value, axis, [(i, i ^ flip) for i in range(lax.axis_size(axis))])


def reduce_parts(value, axis):
    members = lax.axis_size(axis)
    value = value + other(value, axis, 1)
    if members >= 8:
        value = (value + other(value, axis, 2)) + (other(value, axis, 4) + other(value, axis, 6))
    if members >= 32:
        value = value + other(value, axis, 8)
        return (value, other(value, axis, 24))
    return (value, jnp.zeros_like(value))


def on_device(radiance, kernel, w_first, w_mid, w_out, target, mask):
    image = radiance[0]
    bands, rows_all, width = image.shape
    ks = kernel.shape[1]
    peers = lax.axis_size("band")
    crops = lax.axis_size("dp")
    rows = mask.shape[1]
    total, ch = w_first.shape
    scale = 1.0 / math.sqrt(crops * rows_all * width)
    size = round_up(rows * bands, 16)
    taps = jnp.transpose(kernel, (1, 2, 0))
    first = jnp.transpose(w_first, (1, 0))
    wanted = target[0].reshape(total * rows, width)
    spread_wide = round_up(ks * rows_all, LANES)
    params = (image, taps, first, w_mid, w_out, wanted, mask[0])
    filtered, columns, first, w_mid, w_out, wanted, valid = pl.pallas_call(
        spatial_kernel,
        in_specs=[pl.BlockSpec(memory_space=pltpu.HBM)] * len(params),
        out_specs=spots(len(params)),
        out_shape=(pltpu.VMEM((peers, size, width), BF16), pltpu.VMEM((bands, spread_wide, width), BF16))
        + tuple(pltpu.VMEM(p.shape, p.dtype) for p in params[2:]),
        scratch_shapes=[
            pltpu.VMEM(image.shape, BF16),
            pltpu.VMEM(taps.shape, BF16),
            pltpu.VMEM((round_up(bands, 8) + 8, spread_wide), F32),
            pltpu.VMEM((round_up(bands * rows_all, 8) + 8, width), F32),
            pltpu.SemaphoreType.DMA((LOADS + len(params),)),
        ],
        compiler_params=SMALL,
        name="spatial",
    )(*[pltpu.with_memory_space_constraint(p, pltpu.HBM) for p in params])
    spectra = exchange(filtered, "band")
    wide = round_up(2 * total + ch, LANES)
    share_rows = wide // LANES * (ch // peers)
    packed = pl.pallas_call(
        functools.partial(net_kernel, scale=scale),
        in_specs=spots(6),
        out_specs=spots(1)[0],
        out_shape=pltpu.VMEM((peers, size + 2 * share_rows, width), BF16),
        scratch_shapes=[
            pltpu.VMEM((peers * size + 8, width), F32),
            pltpu.VMEM((rows * total + 8, width), F32),
            pltpu.VMEM((ch, wide), F32),
            pltpu.VMEM((rows * total, width), F32),
        ],
        compiler_params=SMALL,
        name="net",
    )(*near(spectra, first, w_mid, w_out, wanted, valid))
    packed = exchange(packed, "band")
    half_up = round_up((bands + 1) // 2, 8)
    sums = pl.pallas_call(
        functools.partial(kernel_grad_kernel, ks=ks, rows=rows_all, size=size),
        in_specs=spots(2),
        out_specs=spots(1)[0],
        out_shape=pltpu.VMEM((share_rows + half_up, width), F32),
        scratch_shapes=[
            pltpu.VMEM((round_up(bands * rows_all, 8) + 8, width), F32),
            pltpu.VMEM((16 * half_up, width), F32),
        ],
        compiler_params=SMALL,
        name="kernel_grad",
    )(*near(columns, packed))
    parts = reduce_parts(sums, "dp")
    shared, own = pl.pallas_call(
        join_kernel,
        in_specs=spots(2),
        out_specs=spots(2),
        out_shape=(pltpu.VMEM((peers, share_rows, width), F32), pltpu.VMEM((half_up, width), F32)),
        compiler_params=SMALL,
        name="join",
    )(*near(*parts))
    shared = exchange(shared, "band")
    grad_kernel, grad_first, grad_mid, grad_out = pl.pallas_call(
        functools.partial(final_kernel, rows=rows_all),
        in_specs=spots(2),
        out_shape=(
            jax.ShapeDtypeStruct((ks, ks, bands), F32),
            jax.ShapeDtypeStruct((ch, total), F32),
            jax.ShapeDtypeStruct((ch, ch), F32),
            jax.ShapeDtypeStruct((ch, total), F32),
        ),
        scratch_shapes=[pltpu.VMEM((LANES + 8, bands), F32), pltpu.VMEM((ch, wide), F32)],
        compiler_params=SMALL,
        name="final",
    )(*near(shared, own))
    return (jnp.transpose(grad_kernel, (2, 0, 1)), jnp.transpose(grad_first, (1, 0)), grad_mid, grad_out)


def solution(mesh):
    in_specs = (
        P("dp", "band", None, None),
        P("band", None, None),
        P(),
        P(),
        P(),
        P("dp", None, "band", None),
        P("dp", "band", None),
    )
    out_specs = (P("band", None, None), P(), P(), P())
    return jax.shard_map(on_device, mesh=mesh, in_specs=in_specs, out_specs=out_specs, check_vma=False)
```
